512 devices in a mesh: rep: 64 (over z, x_lo, core), dom: 8 (over x_hi, y).
Axes of the slice: x: 4 (x_hi: 2, x_lo: 2; x = x_hi * 2 + x_lo), y: 4, z: 16, core: 2. Of those that a mesh axis runs over, the one named last changes fastest.
Arguments:
- particle_locations: float32 [64, 3, 8192], P('rep', None, 'dom'), may hold values from 0 to 1.5
- particle_speeds: float32 [64, 3, 8192], P('rep', None, 'dom'), may hold values from -6 to 6
- current_pushes: float32 [64, 3, 8192], P('rep', None, 'dom'), may hold values from -6 to 6
- particle_kinds: int32 [64, 8192], P('rep', 'dom'), may hold values from 0 to 15
- halo_particle_labels: int32 [64, 6144], P('rep', 'dom'), may hold values from 0 to 1023
- adjacent_block_labels: int32 [64, 64, 4], P('rep', 'dom'), may hold values from 0 to 13
- adjacent_place_totals: int32 [64, 64], P('rep', 'dom'), may hold values from 1 to 4, as said below
- kind_vectors: bfloat16 [16, 128], replicated, may hold values from -6 to 6
- kind_inertia: float32 [16], replicated, may hold values from 1 to 4
- stepwise_distance_coefficients: float32 [2, 8, 128], replicated, may hold values from -2 to 2
- signal_scaling_factors: float32 [2, 128], replicated, may hold values from 0.1 to 1.9
- feature_blend_coefficients: bfloat16 [2, 128, 128], replicated, may hold values from -0.5 to 0.5
- target_projection_array: bfloat16 [128, 128], replicated, may hold values from -0.5 to 0.5
- source_projection_array: bfloat16 [128, 128], replicated, may hold values from -0.5 to 0.5
- push_distance_taper: float32 [8], replicated, may hold values from -4 to 4
- thermal_levels: float32 [64], replicated, may hold values from 0.5 to 2
- granted_swaps: int32 [64], replicated, may hold values from 0 to 63, as said below
Outputs:
- positions_out: float32 [64, 3, 8192], P('rep', None, 'dom')
- velocities_out: float32 [64, 3, 8192], P('rep', None, 'dom')
- forces_out: float32 [64, 3, 8192], P('rep', None, 'dom')
The draws below stay inside these ranges and needn't reach their ends.
Inputs may be any that keep to these rules, and one draw needn't show every extreme that they name: `halo_particle_labels`: each domain's block of 768 entries: the first 384 name its atoms imported by the next lower domain, the last 384 those imported by the next higher domain. `adjacent_block_labels`: numbers below 8 are the domain's own tiles; the rest are the imported atoms' tiles in extended order. `adjacent_place_totals`: in every replica some domain has all its tiles at 4 live slots. `granted_swaps`: each replica's partner is itself or a ladder neighbour, and the partner's partner is the replica. The pairs (0, 1), (31, 32) and (62, 63) are always accepted.
All inputs are finite; a program needn't handle non-finite values.
Results may differ from the reference program's by a relative error of at most 0.0067.
Values may be sent and summed in bfloat16 or wider, within the bound.
A program may use at most 64 MiB of HBM per device.

```python
import math
import jax
import jax.numpy as jnp
from jax import lax

C = 128
NB = 8
SPECIES = 16
TILE = 128
NEI = 4
LAYERS = 2
ATOMS_DEV = 1024
GHOST = 384
TILES_DEV = 8
THERMAL_COPIES = 64
DOMAINS = 8
ATOMS = 8192


def draw_adjacent_place_totals(key, part):
    base_key, dense_key = jax.random.split(key)
    baseline = jax.random.randint(base_key, (THERMAL_COPIES, DOMAINS, TILES_DEV), 1, NEI + 1)
    crowded = jax.random.randint(dense_key, (THERMAL_COPIES, 1, 1), 0, DOMAINS)
    domain_ids = jnp.arange(DOMAINS, dtype=jnp.int32)[None, :, None]
    counts_all = jnp.where(domain_ids == crowded, NEI, baseline)
    return counts_all.reshape(THERMAL_COPIES, DOMAINS * TILES_DEV).astype(jnp.int32)


def draw_granted_swaps(key, part):
    accept_key = jax.random.fold_in(key, 7)
    replica_ids = jnp.arange(THERMAL_COPIES, dtype=jnp.int32)
    half_point = THERMAL_COPIES // 2
    accepted = jax.random.randint(accept_key, (THERMAL_COPIES,), 0, 2)
    forced = (replica_ids == 0) | (replica_ids == half_point - 1) | (replica_ids == THERMAL_COPIES - 2)
    even_free = (replica_ids % 2 == 0) & (replica_ids >= 2) & (replica_ids <= THERMAL_COPIES - 4) & (replica_ids != half_point - 2) & (replica_ids != half_point)
    is_low = forced | even_free & (accepted == 1)
    below_low = jnp.concatenate([jnp.zeros((1,), dtype=bool), is_low[:-1]])
    partner_ids = jnp.where(is_low, replica_ids + 1, jnp.where(below_low, replica_ids - 1, replica_ids))
    return partner_ids.astype(jnp.int32)


def set_ends(values, stream_key, low, largest):
    place = [jax.random.randint(jax.random.fold_in(stream_key, axis), (), 0, length) for axis, length in enumerate(values.shape)]
    widest = values.shape.index(max(values.shape))
    beside = place[:widest] + [(place[widest] + 1) % values.shape[widest]] + place[widest + 1:]
    return values.at[tuple(place)].set(low).at[tuple(beside)].set(largest)


def shard_levels(own_key, shape, shards, smallest, largest):
    factor_of, own = 1.0, jax.random.fold_in(own_key, 6)
    for axis_at, blocks in shards:
        draws = jnp.exp(jax.random.uniform(jax.random.fold_in(own, axis_at), (blocks,), jnp.float32, smallest / len(shards), largest / len(shards)))
        factor_of = factor_of * jnp.repeat(draws, shape[axis_at] // blocks).reshape([-1 if axis == axis_at else 1 for axis in range(len(shape))])
    return factor_of


def normal_values(stream_key, dims, deviation, limit, shards=(), kind=jnp.bfloat16):
    values = deviation * jax.random.normal(stream_key, dims, jnp.float32)
    if shards:
        values = values * shard_levels(stream_key, dims, shards, -0.22, 0.18)
    return jnp.clip(values, -limit, limit).astype(kind)


def setup_inputs(seed: int = 0) -> dict:
    key_of = jax.random.split(jax.random.key(seed), 18)
    return {
        "particle_locations": jnp.clip(1.5 * jax.random.uniform(key_of[0], (THERMAL_COPIES, 3, ATOMS), jnp.float32) ** shard_levels(key_of[0], (THERMAL_COPIES, 3, ATOMS), ((0, 64), (2, 8)), -0.2, 0.2), 0.0, 1.5),
        "particle_speeds": normal_values(key_of[1], (THERMAL_COPIES, 3, ATOMS), 1.0, 6.0, ((0, 64), (2, 8)), jnp.float32),
        "current_pushes": normal_values(key_of[2], (THERMAL_COPIES, 3, ATOMS), 1.0, 6.0, ((0, 64), (2, 8)), jnp.float32),
        "particle_kinds": set_ends(jax.random.randint(key_of[3], (THERMAL_COPIES, ATOMS), 0, SPECIES), jax.random.fold_in(key_of[3], 1), 0, SPECIES - 1).astype(jnp.int32),
        "halo_particle_labels": set_ends(jax.random.randint(key_of[4], (THERMAL_COPIES, 2 * GHOST * DOMAINS), 0, ATOMS_DEV), jax.random.fold_in(key_of[4], 1), 0, ATOMS_DEV - 1).astype(jnp.int32),
        "adjacent_block_labels": set_ends(jax.random.randint(key_of[5], (THERMAL_COPIES, TILES_DEV * DOMAINS, NEI), 0, 7 * TILES_DEV // 4), jax.random.fold_in(key_of[5], 1), 0, (7 * TILES_DEV // 4) - 1).astype(jnp.int32),
        "adjacent_place_totals": draw_adjacent_place_totals(jax.random.fold_in(key_of[17], 71), 0),
        "kind_vectors": normal_values(key_of[7], (SPECIES, C), 1.0, 6.0),
        "kind_inertia": jnp.clip(jnp.exp(jax.random.uniform(key_of[8], (SPECIES,), jnp.float32, math.log(1.0), math.log(4.0))), 1.0, 4.0),
        "stepwise_distance_coefficients": normal_values(key_of[9], (LAYERS, NB, C), NB ** -0.5, 2.0, (), jnp.float32),
        "signal_scaling_factors": jnp.clip(1.0 + 0.18 * jax.random.normal(key_of[10], (LAYERS, C), jnp.float32), 0.1, 1.9),
        "feature_blend_coefficients": normal_values(key_of[11], (LAYERS, C, C), C ** -0.5, 0.5),
        "target_projection_array": normal_values(key_of[12], (C, C), C ** -0.5, 0.5),
        "source_projection_array": normal_values(key_of[13], (C, C), C ** -0.5, 0.5),
        "push_distance_taper": normal_values(key_of[14], (NB,), 1.0, 4.0, (), jnp.float32),
        "thermal_levels": jnp.clip(jnp.exp(jax.random.uniform(key_of[15], (THERMAL_COPIES,), jnp.float32, math.log(0.5), math.log(2.0))), 0.5, 2.0),
        "granted_swaps": draw_granted_swaps(jax.random.fold_in(key_of[17], 71), 0),
    }


slab_width = 1.5
time_step = 0.5
basis_width = 0.3
norm_eps = 1e-06

def pair_basis(near_pos, far_pos, live_flag):
    offsets = far_pos[:, None, :] - near_pos[:, :, None]
    distance = jnp.sqrt(lax.optimization_barrier(jnp.sum(offsets * offsets, axis=0)))
    centers = basis_width * jnp.arange(NB, dtype=jnp.float32)
    scaled = (distance[None, :, :] - centers[:, None, None]) / basis_width
    return (jnp.exp(-scaled * scaled) * live_flag).astype(jnp.bfloat16)

def species_onehot(labels, width):
    return labels[:, None] == jnp.arange(width, dtype=jnp.int32)[None, :]

def embed_rows(labels, kind_vectors):
    onehot = species_onehot(labels, kind_vectors.shape[0]).astype(jnp.bfloat16)
    return jnp.dot(onehot, kind_vectors, preferred_element_type=jnp.float32).astype(jnp.bfloat16)

def tile_messages(ext_pos, ext_hidden, tile_lists, live_counts, radial_row):

    def one_tile(tile_index):
        near_pos = lax.dynamic_slice_in_dim(ext_pos, tile_index * TILE, TILE, 1)
        summed = jnp.zeros((NB, TILE, ext_hidden.shape[1]), jnp.float32)
        for slot_index in range(NEI):
            source = tile_lists[tile_index, slot_index].astype(jnp.int32)
            far_pos = lax.dynamic_slice_in_dim(ext_pos, source * TILE, TILE, 1)
            far_feat = lax.dynamic_slice_in_dim(ext_hidden, source * TILE, TILE, 0)
            live_flag = (slot_index < live_counts[tile_index]).astype(jnp.float32)
            basis_val = pair_basis(near_pos, far_pos, live_flag)
            summed = summed + jnp.einsum('bij,jc->bic', basis_val.astype(jnp.float32), far_feat.astype(jnp.float32), precision=lax.Precision.HIGHEST)
        return jnp.einsum('bic,bc->ic', summed, radial_row, precision=lax.Precision.HIGHEST)
    tile_total = tile_lists.shape[0]
    result = lax.map(one_tile, jnp.arange(tile_total, dtype=jnp.int32))
    return result.reshape(tile_total * TILE, -1)

def refresh(hidden, messages, gain_row, mix_matrix):
    inverse = lax.rsqrt(lax.optimization_barrier(jnp.mean(messages * messages, axis=-1, keepdims=True)) + norm_eps)
    activation = jax.nn.silu(messages * inverse * gain_row).astype(jnp.bfloat16)
    return (hidden.astype(jnp.float32) + jnp.dot(activation, mix_matrix, preferred_element_type=jnp.float32)).astype(jnp.bfloat16)

def tile_forces(ext_pos, query, ext_keys, tile_lists, live_counts, push_distance_taper):
    factor = 1.0 / math.sqrt(query.shape[1] * NEI * TILE)

    def one_tile(tile_index):
        near_pos = lax.dynamic_slice_in_dim(ext_pos, tile_index * TILE, TILE, 1)
        asking = lax.dynamic_slice_in_dim(query, tile_index * TILE, TILE, 0)
        summed = jnp.zeros((3, TILE), jnp.float32)
        for slot_index in range(NEI):
            source = tile_lists[tile_index, slot_index].astype(jnp.int32)
            far_pos = lax.dynamic_slice_in_dim(ext_pos, source * TILE, TILE, 1)
            far_keys = lax.dynamic_slice_in_dim(ext_keys, source * TILE, TILE, 0)
            live_flag = (slot_index < live_counts[tile_index]).astype(jnp.float32)
            basis_val = pair_basis(near_pos, far_pos, live_flag)
            envelope = jnp.einsum('bij,b->ij', basis_val.astype(jnp.float32), push_distance_taper, precision=lax.Precision.HIGHEST)
            scores = jnp.einsum('ic,jc->ij', asking.astype(jnp.float32), far_keys.astype(jnp.float32), precision=lax.Precision.HIGHEST)
            pair_weight = scores * envelope * factor
            summed = summed + jnp.einsum('dj,ij->di', far_pos, pair_weight, precision=lax.Precision.HIGHEST) - near_pos * lax.optimization_barrier(jnp.sum(pair_weight, axis=1))[None, :]
        return summed
    result = lax.map(one_tile, jnp.arange(tile_lists.shape[0], dtype=jnp.int32))
    return jnp.transpose(result, (1, 0, 2)).reshape(3, -1)

def attach(stacked, ghosts, axis_pos):
    packs = jax.vmap(lambda domain_block, domain_rows: jnp.take(domain_block, domain_rows, axis=axis_pos))(stacked, ghosts)
    ghost_count = ghosts.shape[1] // 2
    from_lower = lax.slice_in_dim(jnp.roll(packs, 1, axis=0), ghost_count, 2 * ghost_count, axis=axis_pos + 1)
    from_upper = lax.slice_in_dim(jnp.roll(packs, -1, axis=0), 0, ghost_count, axis=axis_pos + 1)
    return (from_lower, from_upper)

def extend_rows(stacked, ghosts):
    from_lower, from_upper = attach(stacked, ghosts, 0)
    return jnp.concatenate([stacked, from_lower, from_upper], axis=1)

def replica_step(coords, speeds, old_force, labels, ghost_rows, tile_rows, count_rows, weights):
    kind_vectors, kind_inertia, stepwise_distance_coefficients, signal_scaling_factors, feature_blend_coefficients, target_projection_array, source_projection_array, push_distance_taper = weights
    chosen_mass = jnp.where(species_onehot(labels, kind_inertia.shape[0]), kind_inertia[None, :], 0.0)
    inv_mass = 1.0 / lax.optimization_barrier(jnp.sum(chosen_mass, axis=1))
    displaced = coords + time_step * speeds + 0.5 * time_step * time_step * old_force * inv_mass[None, :]
    half_speed = speeds + 0.5 * time_step * old_force * inv_mass[None, :]
    ghosts = ghost_rows.reshape(DOMAINS, 2 * GHOST)
    tile_lists = tile_rows.reshape(DOMAINS, TILES_DEV, NEI)
    live_counts = count_rows.reshape(DOMAINS, TILES_DEV)
    domain_pos = jnp.transpose(displaced.reshape(3, DOMAINS, ATOMS_DEV), (1, 0, 2))
    shift_vec = slab_width * (jnp.arange(3, dtype=jnp.int32) == 0).astype(jnp.float32)[:, None]
    from_lower, from_upper = attach(domain_pos, ghosts, 1)
    ext_pos = jnp.concatenate([domain_pos, from_lower - shift_vec, from_upper + shift_vec], axis=2)
    hidden = embed_rows(labels, kind_vectors).reshape(DOMAINS, ATOMS_DEV, -1)
    for layer_step in range(LAYERS):
        ext_hidden = extend_rows(hidden, ghosts)
        radial_row = stepwise_distance_coefficients[layer_step]
        messages = lax.map(lambda items: tile_messages(items[0], items[1], items[2], items[3], radial_row), (ext_pos, ext_hidden, tile_lists, live_counts))
        hidden = refresh(hidden, messages, signal_scaling_factors[layer_step], feature_blend_coefficients[layer_step])
    query = jnp.dot(hidden, target_projection_array, preferred_element_type=jnp.float32).astype(jnp.bfloat16)
    keys_local = jnp.dot(hidden, source_projection_array, preferred_element_type=jnp.float32).astype(jnp.bfloat16)
    ext_keys = extend_rows(keys_local, ghosts)
    forces = lax.map(lambda items: tile_forces(items[0], items[1], items[2], items[3], items[4], push_distance_taper), (ext_pos, query, ext_keys, tile_lists, live_counts))
    updated_push = jnp.transpose(forces, (1, 0, 2)).reshape(3, ATOMS)
    updated_velocity = half_speed + 0.5 * time_step * updated_push * inv_mass[None, :]
    return (displaced, updated_velocity, updated_push)

def reference(particle_locations, particle_speeds, current_pushes, particle_kinds, halo_particle_labels, adjacent_block_labels, adjacent_place_totals, kind_vectors, kind_inertia, stepwise_distance_coefficients, signal_scaling_factors, feature_blend_coefficients, target_projection_array, source_projection_array, push_distance_taper, thermal_levels, granted_swaps):
    weights = (kind_vectors, kind_inertia, stepwise_distance_coefficients, signal_scaling_factors, feature_blend_coefficients, target_projection_array, source_projection_array, push_distance_taper)

    def per_replica(items):
        return replica_step(items[0], items[1], items[2], items[3], items[4], items[5], items[6], weights)
    displaced, updated_velocity, updated_push = lax.map(per_replica, (particle_locations, particle_speeds, current_pushes, particle_kinds, halo_particle_labels, adjacent_block_labels, adjacent_place_totals))
    thermal_quotient = jnp.sqrt(thermal_levels / thermal_levels[granted_swaps])
    return (displaced[granted_swaps], updated_velocity[granted_swaps] * thermal_quotient[:, None, None], updated_push[granted_swaps])
```

```python
import math

import jax
import jax.numpy as jnp
from jax import lax
from jax.experimental import pallas as pl
from jax.experimental.pallas import tpu as pltpu
from jax.sharding import PartitionSpec as P

NB = 8
TILE = 128
NEI = 4
TILES = 8
GT = 3
EXT = TILES + 2 * GT
ATOMS = TILES * TILE
SPECIES = 16
CH = 128
CHUNK = 32

slab_width = 1.5
time_step = 0.5
basis_width = 0.3
norm_eps = 1e-06
factor = 1.0 / math.sqrt(CH * NEI * TILE)

ROOT = math.sqrt(math.log2(math.e))
SCALE = ROOT / basis_width
TOP = (NB - 1) * ROOT
FAR = 1.0e3

MESH = pl.DeviceIdType.MESH


def columns(row):
    return jnp.broadcast_to(row, (TILE, TILE)).T


def pick(offset, own, low, high):
    return jnp.where(offset == 1, high, jnp.where(offset == -1, low, own))


def step_kernel(
    reps,
    doms,
    loc_ref,
    spd_ref,
    frc_ref,
    kind_ref,
    ghost_ref,
    adj_ref,
    live_ref,
    vec_ref,
    inertia_ref,
    radial_ref,
    gain_ref,
    mix_ref,
    target_ref,
    source_ref,
    taper_ref,
    heat_ref,
    swap_ref,
    pos_out,
    vel_out,
    frc_out,
    posext,
    psend,
    xcol,
    hext,
    mid,
    keys,
    hsend,
    onehot,
    basis,
    env,
    hcat,
    scores,
    facc,
    last,
    query,
    state,
    state_in,
    fown,
    f_in,
    send_sem,
    recv_sem,
):
    rep = lax.axis_index("rep")
    dom = lax.axis_index("dom")
    rep_to = (lax.rem(rep + 1, reps), lax.rem(rep + reps - 1, reps))
    dom_to = (lax.rem(dom + 1, doms), lax.rem(dom + doms - 1, doms))

    barrier = pltpu.get_barrier_semaphore()
    for side in range(2):
        pl.semaphore_signal(barrier, inc=1, device_id={"dom": dom_to[side]}, device_id_type=MESH)
        pl.semaphore_signal(barrier, inc=1, device_id={"rep": rep_to[side]}, device_id_type=MESH)

    def copy(stage, side, axis, src, dst):
        to = dom_to[side] if axis == "dom" else rep_to[side]
        return pltpu.make_async_remote_copy(
            src_ref=src,
            dst_ref=dst,
            send_sem=send_sem.at[2 * stage + side],
            recv_sem=recv_sem.at[2 * stage + side],
            device_id={axis: to},
            device_id_type=MESH,
        )

    kinds = kind_ref[...]
    mass = jnp.zeros((1, ATOMS), jnp.float32)
    for s in range(SPECIES):
        mass = jnp.where(kinds == s, inertia_ref[s], mass)
    inv_mass = 1.0 / mass
    loc, spd, frc = loc_ref[0], spd_ref[0], frc_ref[0]
    moved = loc + time_step * spd + 0.5 * time_step * time_step * frc * inv_mass
    half = spd + 0.5 * time_step * frc * inv_mass
    kindf = kinds.astype(jnp.float32)
    for t in range(TILES):
        lanes = slice(t * TILE, (t + 1) * TILE)
        posext[t] = jnp.zeros((8, TILE), jnp.float32)
        posext[t, 0:3, :] = moved[:, lanes]
        posext[t, 3:4, :] = kindf[:, lanes]

    first_row = lax.broadcasted_iota(jnp.int32, (8, TILE), 0) == 0
    for side in range(2):
        for g in range(GT):
            start = ((1 - side) * GT + g) * TILE
            label = jnp.broadcast_to(ghost_ref[:, start : start + TILE], (8, TILE))
            place = label & (TILE - 1)
            owner = label >> 7
            out = jnp.zeros((8, TILE), jnp.float32)
            for t in range(TILES):
                got = jnp.take_along_axis(posext[t], place, axis=1, mode="promise_in_bounds")
                out = jnp.where(owner == t, got, out)
            shift = slab_width if side == 1 else -slab_width
            psend[side, g] = jnp.where(first_row, out + shift, out)

    pl.semaphore_wait(barrier, 4)
    pos_copies = [
        copy(0, side, "dom", psend.at[side], posext.at[pl.ds(TILES + GT * side, GT)])
        for side in range(2)
    ]
    for c in pos_copies:
        c.start()

    state[0:3, :] = moved
    state[3:6, :] = half
    state[6:7, :] = inv_mass
    state[7:8, :] = inv_mass
    state_copies = [copy(1, side, "rep", state, state_in.at[side]) for side in range(2)]
    for c in state_copies:
        c.start()

    lane = lax.broadcasted_iota(jnp.int32, (TILE, TILE), 1)
    lanef = lane.astype(jnp.float32)
    vectors = jnp.concatenate([vec_ref[...], jnp.zeros((TILE - SPECIES, CH), jnp.bfloat16)], axis=0)

    def embed(s):
        hot = jnp.where(columns(posext[s, 3:4, :]) == lanef, 1.0, 0.0).astype(jnp.bfloat16)
        hext[s] = jnp.dot(hot, vectors, preferred_element_type=jnp.float32).astype(jnp.bfloat16)

    def own_tile(t, _):
        for axis in range(3):
            xcol[t, axis] = columns(posext[t, axis : axis + 1, :])
        embed(t)
        return 0

    lax.fori_loop(0, TILES, own_tile, 0)

    for g in range(2 * GT):
        labels = columns(ghost_ref[:, g * TILE : (g + 1) * TILE])
        for t in range(TILES):
            hot = jnp.where(labels == lane + t * TILE, 1.0, 0.0).astype(jnp.bfloat16)
            onehot[g * TILE : (g + 1) * TILE, t * TILE : (t + 1) * TILE] = hot

    for c in pos_copies:
        c.wait()

    def ghost_tile(s, _):
        embed(s)
        return 0

    lax.fori_loop(TILES, EXT, ghost_tile, 0)

    def fill_basis(t):
        for k in range(NEI):
            far = posext[adj_ref[0, t, k]]
            dead = jnp.clip(k + 1 - live_ref[0, t], 0, 1).astype(jnp.float32) * FAR
            xj, yj, zj = far[0:1, :] + dead, far[1:2, :], far[2:3, :]
            for c in range(TILE // CHUNK):
                rows = slice(c * CHUNK, (c + 1) * CHUNK)
                dx = xj - xcol[t, 0, rows, :]
                dy = yj - xcol[t, 1, rows, :]
                dz = zj - xcol[t, 2, rows, :]
                square = dx * dx + dy * dy + dz * dz
                a = square * lax.rsqrt(jnp.maximum(square, 1e-30)) * SCALE
                top = a - TOP
                g = jnp.exp2(-(top * top))
                q = jnp.exp2(a * (-2.0 * ROOT))
                for b in range(NB - 1, -1, -1):
                    basis[t, b, rows, k * TILE : (k + 1) * TILE] = g.astype(jnp.bfloat16)
                    if b:
                        g = g * (q * math.exp(2 * b - 1))

    def layer_tile(layer, t, source):
        for k in range(NEI):
            hcat[k * TILE : (k + 1) * TILE, :] = source[adj_ref[0, t, k]]
        summed = jnp.dot(
            basis[t].reshape(NB * TILE, NEI * TILE), hcat[...], preferred_element_type=jnp.float32
        )
        radial = radial_ref[layer]
        messages = radial[0:1, :] * summed[0:TILE, :]
        for b in range(1, NB):
            messages = messages + radial[b : b + 1, :] * summed[b * TILE : (b + 1) * TILE, :]
        inverse = lax.rsqrt(jnp.mean(messages * messages, axis=-1, keepdims=True) + norm_eps)
        scaled = messages * inverse * gain_ref[layer : layer + 1, :]
        activation = (scaled / (1.0 + jnp.exp(-scaled))).astype(jnp.bfloat16)
        return (
            source[t].astype(jnp.float32)
            + jnp.dot(activation, mix_ref[layer], preferred_element_type=jnp.float32)
        ).astype(jnp.bfloat16)

    def first_layer(t, _):
        fill_basis(t)
        mid[t] = layer_tile(0, t, hext)
        return 0

    lax.fori_loop(0, TILES, first_layer, 0)

    def export(stage, rows, buffer, slot):
        copies = []
        for side in range(2):
            start = (1 - side) * GT * TILE
            packed = jnp.dot(
                onehot[start : start + GT * TILE, :], rows, preferred_element_type=jnp.float32
            )
            hsend[slot, side] = packed.astype(jnp.bfloat16).reshape(GT, TILE, CH)
            c = copy(
                stage, side, "dom", hsend.at[slot, side], buffer.at[pl.ds(TILES + GT * side, GT)]
            )
            c.start()
            copies.append(c)
        return copies

    mid_copies = export(2, mid[0:TILES].reshape(ATOMS, CH), mid, 0)

    def fill_env(t, _):
        for c in range(TILE // CHUNK):
            rows = slice(c * CHUNK, (c + 1) * CHUNK)
            total = taper_ref[0] * basis[t, 0, rows, :].astype(jnp.float32)
            for b in range(1, NB):
                total = total + taper_ref[b] * basis[t, b, rows, :].astype(jnp.float32)
            env[t, rows, :] = total * factor
        return 0

    lax.fori_loop(0, TILES, fill_env, 0)

    for c in mid_copies:
        c.wait()

    def second_layer(t, _):
        hidden = layer_tile(1, t, mid)
        last[t] = hidden
        keys[t] = jnp.dot(
            hidden, source_ref[...], preferred_element_type=jnp.float32
        ).astype(jnp.bfloat16)
        return 0

    lax.fori_loop(0, TILES, second_layer, 0)
    key_copies = export(3, keys[0:TILES].reshape(ATOMS, CH), keys, 1)

    query[...] = (
        jnp.dot(
            last[...].reshape(ATOMS, CH), target_ref[...], preferred_element_type=jnp.float32
        )
        .astype(jnp.bfloat16)
        .reshape(TILES, TILE, CH)
    )
    for c in state_copies:
        c.wait()
    partner = swap_ref[rep]
    offset = jnp.full((3, ATOMS), partner - rep, jnp.int32)
    own_state, low_state, high_state = state[...], state_in[0], state_in[1]
    pos_out[0] = pick(offset, own_state[0:3], low_state[0:3], high_state[0:3])
    half_of = pick(offset, own_state[3:6], low_state[3:6], high_state[3:6])
    inv_of = pick(offset[0:1], own_state[6:7], low_state[6:7], high_state[6:7])
    quotient = jnp.sqrt(
        jnp.full((1, ATOMS), heat_ref[rep], jnp.float32)
        / jnp.full((1, ATOMS), heat_ref[partner], jnp.float32)
    )

    for c in key_copies:
        c.wait()

    def force_tile(t, _):
        for k in range(NEI):
            hcat[k * TILE : (k + 1) * TILE, :] = keys[adj_ref[0, t, k]]
        scores[...] = lax.dot_general(
            query[t], hcat[...], (((1,), (1,)), ((), ())), preferred_element_type=jnp.float32
        )
        fars = [posext[adj_ref[0, t, k]] for k in range(NEI)]
        for c in range(TILE // CHUNK):
            rows = slice(c * CHUNK, (c + 1) * CHUNK)
            weights = scores[rows, :] * env[t, rows, :]
            for axis in range(3):
                near = xcol[t, axis, rows, :]
                total = jnp.zeros((CHUNK, TILE), jnp.float32)
                for k in range(NEI):
                    weight = weights[:, k * TILE : (k + 1) * TILE]
                    total = total + weight * (fars[k][axis : axis + 1, :] - near)
                facc[axis, rows, :] = total
        for axis in range(3):
            fown[axis : axis + 1, pl.ds(pl.multiple_of(t * TILE, TILE), TILE)] = jnp.sum(
                facc[axis].T, axis=0, keepdims=True
            )
        return 0

    lax.fori_loop(0, TILES, force_tile, 0)

    f_copies = [copy(4, side, "rep", fown, f_in.at[side]) for side in range(2)]
    for c in f_copies:
        c.start()
    for c in f_copies:
        c.wait()
    force = pick(offset, fown[...], f_in[0], f_in[1])
    frc_out[0] = force
    vel_out[0] = (half_of + 0.5 * time_step * force * inv_of) * quotient


def solution(mesh):
    reps, doms = mesh.shape["rep"], mesh.shape["dom"]

    def kernel(*refs):
        step_kernel(reps, doms, *refs)

    def local(*args):
        vmem = pl.BlockSpec(memory_space=pltpu.VMEM)
        smem = pl.BlockSpec(memory_space=pltpu.SMEM)
        out = jax.ShapeDtypeStruct((1, 3, ATOMS), jnp.float32)
        f32, bf16 = jnp.float32, jnp.bfloat16
        return pl.pallas_call(
            kernel,
            out_shape=(out, out, out),
            in_specs=[
                vmem, vmem, vmem, vmem, vmem, smem, smem, vmem, smem,
                vmem, vmem, vmem, vmem, vmem, smem, smem, smem,
            ],
            out_specs=(vmem, vmem, vmem),
            scratch_shapes=[
                pltpu.VMEM((EXT, 8, TILE), f32),
                pltpu.VMEM((2, GT, 8, TILE), f32),
                pltpu.VMEM((TILES, 3, TILE, TILE), f32),
                pltpu.VMEM((EXT, TILE, CH), bf16),
                pltpu.VMEM((EXT, TILE, CH), bf16),
                pltpu.VMEM((EXT, TILE, CH), bf16),
                pltpu.VMEM((2, 2, GT, TILE, CH), bf16),
                pltpu.VMEM((2 * GT * TILE, ATOMS), bf16),
                pltpu.VMEM((TILES, NB, TILE, NEI * TILE), bf16),
                pltpu.VMEM((TILES, TILE, NEI * TILE), f32),
                pltpu.VMEM((NEI * TILE, CH), bf16),
                pltpu.VMEM((TILE, NEI * TILE), f32),
                pltpu.VMEM((3, TILE, TILE), f32),
                pltpu.VMEM((TILES, TILE, CH), bf16),
                pltpu.VMEM((TILES, TILE, CH), bf16),
                pltpu.VMEM((8, ATOMS), f32),
                pltpu.VMEM((2, 8, ATOMS), f32),
                pltpu.VMEM((3, ATOMS), f32),
                pltpu.VMEM((2, 3, ATOMS), f32),
                pltpu.SemaphoreType.DMA((10,)),
                pltpu.SemaphoreType.DMA((10,)),
            ],
            compiler_params=pltpu.CompilerParams(
                collective_id=0, has_side_effects=True, vmem_limit_bytes=48 * 1024 * 1024
            ),
            name="md_step",
        )(*args)

    in_specs = (
        P("rep", None, "dom"),
        P("rep", None, "dom"),
        P("rep", None, "dom"),
        P("rep", "dom"),
        P("rep", "dom"),
        P("rep", "dom", None),
        P("rep", "dom"),
        P(), P(), P(), P(), P(), P(), P(), P(), P(), P(),
    )
    out_specs = (P("rep", None, "dom"), P("rep", None, "dom"), P("rep", None, "dom"))
    return jax.shard_map(local, mesh=mesh, in_specs=in_specs, out_specs=out_specs, check_vma=False)
```

```python
import math

import jax
import jax.numpy as jnp
from jax import lax
from jax.experimental import pallas as pl
from jax.experimental.pallas import tpu as pltpu
from jax.sharding import PartitionSpec as P

NB = 8
TILE = 128
NEI = 4
TILES = 8
GT = 3
EXT = TILES + 2 * GT
ATOMS = TILES * TILE
SPECIES = 16
CH = 128
CHUNK = 32

slab_width = 1.5
time_step = 0.5
basis_width = 0.3
norm_eps = 1e-06
factor = 1.0 / math.sqrt(CH * NEI * TILE)

ROOT = math.sqrt(math.log2(math.e))
SCALE = ROOT / basis_width
TOP = (NB - 1) * ROOT
FAR = 1.0e3

MESH = pl.DeviceIdType.MESH


def columns(row):
    return jnp.broadcast_to(row, (TILE, TILE)).T


def pick(offset, own, low, high):
    return jnp.where(offset == 1, high, jnp.where(offset == -1, low, own))


def step_kernel(reps, doms, *refs):
    ins, refs = refs[:17], refs[17:]
    (pos_out, vel_out, frc_out), refs = refs[:3], refs[3:]
    held, refs = refs[:17], refs[17:]
    (
        loc_ref, spd_ref, frc_ref, kind_ref, ghost_ref, adj_ref, live_ref, vec_ref, inertia_ref,
        radial_ref, gain_ref, mix_ref, target_ref, source_ref, taper_ref, heat_ref, swap_ref,
    ) = held
    (
        posext, psend, xcol, hext, mid, keys, hsend, onehot, even, odd, env, hcat, msgs,
        scores, facc, last, query, state, state_in, fown, f_in, in_sem, send_sem, recv_sem,
    ) = refs
    rep = lax.axis_index("rep")
    dom = lax.axis_index("dom")
    rep_to = (rep + 1, rep - 1)
    has = (rep < reps - 1, rep > 0)
    dom_to = (lax.rem(dom + 1, doms), lax.rem(dom + doms - 1, doms))

    barrier = pltpu.get_barrier_semaphore()
    for side in range(2):
        pl.semaphore_signal(barrier, inc=1, device_id={"dom": dom_to[side]}, device_id_type=MESH)

        @pl.when(has[side])
        def _():
            pl.semaphore_signal(
                barrier, inc=1, device_id={"rep": rep_to[side]}, device_id_type=MESH
            )

    loads = [
        pltpu.make_async_copy(ins[i], held[i], in_sem.at[i]) for i in range(17)
    ]
    for c in loads:
        c.start()

    def copy(stage, side, axis, src, dst):
        to = dom_to[side] if axis == "dom" else rep_to[side]
        return pltpu.make_async_remote_copy(
            src_ref=src,
            dst_ref=dst,
            send_sem=send_sem.at[2 * stage + side],
            recv_sem=recv_sem.at[2 * stage + side],
            device_id={axis: to},
            device_id_type=MESH,
        )

    def ladder_start(copies):
        for side in range(2):
            pl.when(has[side])(copies[side].start)

    def ladder_wait(copies):
        for side in range(2):
            pl.when(has[side])(copies[side].wait_send)
            pl.when(has[1 - side])(copies[side].wait_recv)

    for i in (8, 3, 0, 1, 2):
        loads[i].wait()
    kinds = kind_ref[...]
    mass = jnp.zeros((1, ATOMS), jnp.float32)
    for s in range(SPECIES):
        mass = jnp.where(kinds == s, inertia_ref[s], mass)
    inv_mass = 1.0 / mass
    moved, half = [], []
    for axis in range(3):
        loc, spd, frc = loc_ref[axis], spd_ref[axis], frc_ref[axis]
        moved.append(loc + time_step * spd + 0.5 * time_step * time_step * frc * inv_mass)
        half.append(spd + 0.5 * time_step * frc * inv_mass)
    kindf = kinds.astype(jnp.float32)
    for t in range(TILES):
        lanes = slice(t * TILE, (t + 1) * TILE)
        posext[t] = jnp.zeros((8, TILE), jnp.float32)
        for axis in range(3):
            posext[t, axis : axis + 1, :] = moved[axis][:, lanes]
        posext[t, 3:4, :] = kindf[:, lanes]

    loads[4].wait()
    first_row = lax.broadcasted_iota(jnp.int32, (8, TILE), 0) == 0
    for side in range(2):
        for g in range(GT):
            start = ((1 - side) * GT + g) * TILE
            label = jnp.broadcast_to(ghost_ref[:, start : start + TILE], (8, TILE))
            place = label & (TILE - 1)
            owner = label >> 7
            out = jnp.zeros((8, TILE), jnp.float32)
            for t in range(TILES):
                got = jnp.take_along_axis(posext[t], place, axis=1, mode="promise_in_bounds")
                out = jnp.where(owner == t, got, out)
            shift = slab_width if side == 1 else -slab_width
            psend[side, g] = jnp.where(first_row, out + shift, out)

    pl.semaphore_wait(barrier, 2 + has[0].astype(jnp.int32) + has[1].astype(jnp.int32))
    pos_copies = [
        copy(0, side, "dom", psend.at[side], posext.at[pl.ds(TILES + GT * side, GT)])
        for side in range(2)
    ]
    for c in pos_copies:
        c.start()

    for axis in range(3):
        state[axis] = moved[axis]
        state[3 + axis] = half[axis]
    state[6] = inv_mass
    state_copies = [copy(1, side, "rep", state, state_in.at[side]) for side in range(2)]
    ladder_start(state_copies)
    for side in range(2):

        @pl.when(jnp.logical_not(has[1 - side]))
        def _():
            state_in[side] = jnp.zeros((7, 1, ATOMS), jnp.float32)
            f_in[side] = jnp.zeros((3, 1, ATOMS), jnp.float32)

    lane = lax.broadcasted_iota(jnp.int32, (TILE, TILE), 1)
    lanef = lane.astype(jnp.float32)
    loads[7].wait()
    vectors = jnp.concatenate([vec_ref[...], jnp.zeros((TILE - SPECIES, CH), jnp.bfloat16)], axis=0)

    def embed(s):
        hot = jnp.where(columns(posext[s, 3:4, :]) == lanef, 1.0, 0.0).astype(jnp.bfloat16)
        hext[s] = jnp.dot(hot, vectors, preferred_element_type=jnp.float32).astype(jnp.bfloat16)

    def own_tile(t, _):
        for axis in range(3):
            xcol[t, axis] = columns(posext[t, axis : axis + 1, :])
        embed(t)
        return 0

    lax.fori_loop(0, TILES, own_tile, 0)

    for g in range(2 * GT):
        labels = columns(ghost_ref[:, g * TILE : (g + 1) * TILE])
        for t in range(TILES):
            hot = jnp.where(labels == lane + t * TILE, 1.0, 0.0).astype(jnp.bfloat16)
            onehot[t, g * TILE : (g + 1) * TILE, :] = hot

    for i in (5, 6, 9, 10, 11, 12, 13, 14, 15, 16):
        loads[i].wait()
    for c in pos_copies:
        c.wait()

    def fill_basis(t, buffer, slot):
        for k in range(NEI):
            far = posext[adj_ref[0, k, t]]
            dead = jnp.clip(k + 1 - live_ref[0, t], 0, 1).astype(jnp.float32) * FAR
            xj, yj, zj = far[0:1, :] + dead, far[1:2, :], far[2:3, :]
            for c in range(TILE // CHUNK):
                rows = slice(c * CHUNK, (c + 1) * CHUNK)
                dx = xj - xcol[t, 0, rows, :]
                dy = yj - xcol[t, 1, rows, :]
                dz = zj - xcol[t, 2, rows, :]
                square = dx * dx + dy * dy + dz * dz
                a = square * lax.rsqrt(jnp.maximum(square, 1e-30)) * SCALE
                top = a - TOP
                g = jnp.exp2(top * (TOP - a))
                q = jnp.exp2(a * (-2.0 * ROOT))
                for b in range(NB - 1, -1, -1):
                    buffer[slot, k, b, rows, :] = g.astype(jnp.bfloat16)
                    if b:
                        g = g * (q * math.exp(2 * b - 1))

    def sum_messages(layer, t, buffer, slot, source, parity):
        for k in range(NEI):
            hcat[parity, k * TILE : (k + 1) * TILE, :] = source[adj_ref[0, k, t]]
        flat = jnp.concatenate(
            [buffer[slot, k].reshape(NB * TILE, TILE) for k in range(NEI)], axis=1
        )
        summed = jnp.dot(flat, hcat[parity], preferred_element_type=jnp.float32)
        radial = radial_ref[layer]
        messages = radial[0:1, :] * summed[0:TILE, :]
        for b in range(1, NB):
            messages = messages + radial[b : b + 1, :] * summed[b * TILE : (b + 1) * TILE, :]
        msgs[parity] = messages

    def refresh(layer, t, source, parity):
        messages = msgs[parity]
        inverse = lax.rsqrt(jnp.mean(messages * messages, axis=-1, keepdims=True) + norm_eps)
        scaled = messages * inverse * gain_ref[layer : layer + 1, :]
        activation = (scaled / (1.0 + jnp.exp(-scaled))).astype(jnp.bfloat16)
        return (
            source[t].astype(jnp.float32)
            + jnp.dot(activation, mix_ref[layer], preferred_element_type=jnp.float32)
        ).astype(jnp.bfloat16)

    halves = (even, odd)

    def fill(t, u, parity):
        fill_basis(t, halves[parity], u)

    def run_layer(layer, source, finish, prepare):
        def gather(t, u, parity):
            sum_messages(layer, t, halves[parity], u, source, parity)

        def end(t, parity):
            finish(t, refresh(layer, t, source, parity))

        if prepare:
            fill(1, 0, 1)
        gather(0, 0, 0)

        def pair(u, _):
            if prepare:
                fill(2 * u + 2, u + 1, 0)
            gather(2 * u + 1, u, 1)
            end(2 * u, 0)
            if prepare:
                fill(2 * u + 3, u + 1, 1)
            gather(2 * u + 2, u + 1, 0)
            end(2 * u + 1, 1)
            return 0

        lax.fori_loop(0, TILES // 2 - 1, pair, 0)
        gather(TILES - 1, TILES // 2 - 1, 1)
        end(TILES - 2, 0)
        end(TILES - 1, 1)

    fill(0, 0, 0)
    for s in range(TILES, EXT):
        embed(s)

    def keep_mid(t, hidden):
        mid[t] = hidden

    run_layer(0, hext, keep_mid, True)

    def export(stage, rows, buffer, slot):
        copies = []
        for side in range(2):
            start = (1 - side) * GT * TILE
            hot = jnp.concatenate(
                [onehot[t, start : start + GT * TILE, :] for t in range(TILES)], axis=1
            )
            packed = jnp.dot(hot, rows, preferred_element_type=jnp.float32)
            hsend[slot, side] = packed.astype(jnp.bfloat16).reshape(GT, TILE, CH)
            c = copy(
                stage, side, "dom", hsend.at[slot, side], buffer.at[pl.ds(TILES + GT * side, GT)]
            )
            c.start()
            copies.append(c)
        return copies

    mid_copies = export(2, mid[0:TILES].reshape(ATOMS, CH), mid, 0)

    def fill_env(u, _):
        for parity in range(2):
            for k in range(NEI):
                total = taper_ref[0] * halves[parity][u, k, 0].astype(jnp.float32)
                for b in range(1, NB):
                    total = total + taper_ref[b] * halves[parity][u, k, b].astype(jnp.float32)
                env[2 * u + parity, k] = total * factor
        return 0

    lax.fori_loop(0, TILES // 2, fill_env, 0)

    for c in mid_copies:
        c.wait()

    def keep_last(t, hidden):
        last[t] = hidden
        keys[t] = jnp.dot(
            hidden, source_ref[...], preferred_element_type=jnp.float32
        ).astype(jnp.bfloat16)

    run_layer(1, mid, keep_last, False)
    key_copies = export(3, keys[0:TILES].reshape(ATOMS, CH), keys, 1)

    query[...] = (
        jnp.dot(
            last[...].reshape(ATOMS, CH), target_ref[...], preferred_element_type=jnp.float32
        )
        .astype(jnp.bfloat16)
        .reshape(TILES, TILE, CH)
    )
    ladder_wait(state_copies)
    partner = swap_ref[rep]
    offset = jnp.full((1, ATOMS), partner - rep, jnp.int32)
    for axis in range(3):
        pos_out[axis] = pick(offset, state[axis], state_in[0, axis], state_in[1, axis])
    quotient = jnp.sqrt(
        jnp.full((1, ATOMS), heat_ref[rep], jnp.float32)
        / jnp.full((1, ATOMS), heat_ref[partner], jnp.float32)
    )

    for c in key_copies:
        c.wait()

    def force_pair(u, _):
        for parity in range(2):
            t = 2 * u + parity
            for k in range(NEI):
                hcat[parity, k * TILE : (k + 1) * TILE, :] = keys[adj_ref[0, k, t]]
            scores[parity] = lax.dot_general(
                query[t],
                hcat[parity],
                (((1,), (1,)), ((), ())),
                preferred_element_type=jnp.float32,
            )
            fars = [posext[adj_ref[0, k, t]] for k in range(NEI)]
            for c in range(TILE // CHUNK):
                rows = slice(c * CHUNK, (c + 1) * CHUNK)
                weights = [
                    scores[parity, rows, k * TILE : (k + 1) * TILE] * env[t, k, rows, :]
                    for k in range(NEI)
                ]
                for axis in range(3):
                    near = xcol[t, axis, rows, :]
                    total = weights[0] * (fars[0][axis : axis + 1, :] - near)
                    for k in range(1, NEI):
                        total = total + weights[k] * (fars[k][axis : axis + 1, :] - near)
                    facc[parity, axis, rows, :] = total
            for axis in range(3):
                fown[axis, :, pl.ds(pl.multiple_of(t * TILE, TILE), TILE)] = jnp.sum(
                    facc[parity, axis].T, axis=0, keepdims=True
                )
        return 0

    lax.fori_loop(0, TILES // 2, force_pair, 0)

    f_copies = [copy(4, side, "rep", fown, f_in.at[side]) for side in range(2)]
    ladder_start(f_copies)
    ladder_wait(f_copies)
    inv_of = pick(offset, state[6], state_in[0, 6], state_in[1, 6])
    for axis in range(3):
        force = pick(offset, fown[axis], f_in[0, axis], f_in[1, axis])
        half_of = pick(offset, state[3 + axis], state_in[0, 3 + axis], state_in[1, 3 + axis])
        frc_out[axis] = force
        vel_out[axis] = (half_of + 0.5 * time_step * force * inv_of) * quotient


def solution(mesh):
    reps, doms = mesh.shape["rep"], mesh.shape["dom"]

    def kernel(*refs):
        step_kernel(reps, doms, *refs)

    def local(*args):
        args = list(args)
        for i in range(3):
            args[i] = jnp.transpose(args[i], (1, 0, 2))
        args[5] = jnp.transpose(args[5], (0, 2, 1))
        vmem = pl.BlockSpec(memory_space=pltpu.VMEM)
        hbm = pl.BlockSpec(memory_space=pltpu.HBM)
        out = jax.ShapeDtypeStruct((3, 1, ATOMS), jnp.float32)
        f32, bf16 = jnp.float32, jnp.bfloat16
        scalar = (5, 6, 8, 14, 15, 16)
        held = [
            (pltpu.SMEM if i in scalar else pltpu.VMEM)(x.shape, x.dtype)
            for i, x in enumerate(args)
        ]
        outs = pl.pallas_call(
            kernel,
            out_shape=(out, out, out),
            in_specs=[hbm] * 17,
            out_specs=(vmem, vmem, vmem),
            scratch_shapes=held
            + [
                pltpu.VMEM((EXT, 8, TILE), f32),
                pltpu.VMEM((2, GT, 8, TILE), f32),
                pltpu.VMEM((TILES, 3, TILE, TILE), f32),
                pltpu.VMEM((EXT, TILE, CH), bf16),
                pltpu.VMEM((EXT, TILE, CH), bf16),
                pltpu.VMEM((EXT, TILE, CH), bf16),
                pltpu.VMEM((2, 2, GT, TILE, CH), bf16),
                pltpu.VMEM((TILES, 2 * GT * TILE, TILE), bf16),
                pltpu.VMEM((TILES // 2, NEI, NB, TILE, TILE), bf16),
                pltpu.VMEM((TILES // 2, NEI, NB, TILE, TILE), bf16),
                pltpu.VMEM((TILES, NEI, TILE, TILE), f32),
                pltpu.VMEM((2, NEI * TILE, CH), bf16),
                pltpu.VMEM((2, TILE, CH), f32),
                pltpu.VMEM((2, TILE, NEI * TILE), f32),
                pltpu.VMEM((2, 3, TILE, TILE), f32),
                pltpu.VMEM((TILES, TILE, CH), bf16),
                pltpu.VMEM((TILES, TILE, CH), bf16),
                pltpu.VMEM((7, 1, ATOMS), f32),
                pltpu.VMEM((2, 7, 1, ATOMS), f32),
                pltpu.VMEM((3, 1, ATOMS), f32),
                pltpu.VMEM((2, 3, 1, ATOMS), f32),
                pltpu.SemaphoreType.DMA((17,)),
                pltpu.SemaphoreType.DMA((10,)),
                pltpu.SemaphoreType.DMA((10,)),
            ],
            compiler_params=pltpu.CompilerParams(
                collective_id=0, has_side_effects=True, vmem_limit_bytes=67043328
            ),
            name="md_step",
        )(*args)
        return tuple(jnp.transpose(x, (1, 0, 2)) for x in outs)

    in_specs = (
        P("rep", None, "dom"),
        P("rep", None, "dom"),
        P("rep", None, "dom"),
        P("rep", "dom"),
        P("rep", "dom"),
        P("rep", "dom", None),
        P("rep", "dom"),
        P(), P(), P(), P(), P(), P(), P(), P(), P(), P(),
    )
    out_specs = (P("rep", None, "dom"), P("rep", None, "dom"), P("rep", None, "dom"))
    return jax.shard_map(local, mesh=mesh, in_specs=in_specs, out_specs=out_specs, check_vma=False)
```

```python
import math

import jax
import jax.numpy as jnp
from jax import lax
from jax.experimental import pallas as pl
from jax.experimental.pallas import tpu as pltpu
from jax.sharding import PartitionSpec as P

NB = 8
TILE = 128
NEI = 4
TILES = 8
GT = 3
EXT = TILES + 2 * GT
ATOMS = TILES * TILE
SPECIES = 16
CH = 128
CHUNK = 32

slab_width = 1.5
time_step = 0.5
basis_width = 0.3
norm_eps = 1e-06
factor = 1.0 / math.sqrt(CH * NEI * TILE)

ROOT = math.sqrt(math.log2(math.e))
SCALE = ROOT / basis_width
TOP = (NB - 1) * ROOT
FAR = 1.0e3
UNFOLD = [math.exp((NB - 1) ** 2 - b * b) for b in range(NB)]

MESH = pl.DeviceIdType.MESH


def columns(row):
    return jnp.broadcast_to(row, (TILE, TILE)).T


def pick(offset, own, low, high):
    return jnp.where(offset == 1, high, jnp.where(offset == -1, low, own))


def step_kernel(reps, doms, *refs):
    ins, refs = refs[:17], refs[17:]
    (result,), refs = refs[:1], refs[1:]
    held, refs = refs[:17], refs[17:]
    (
        loc_ref, spd_ref, frc_ref, kind_ref, ghost_ref, adj_ref, live_ref, vec_ref, inertia_ref,
        radial_ref, gain_ref, mix_ref, target_ref, source_ref, taper_ref, heat_ref, swap_ref,
    ) = held
    (
        posext, psend, xcol, hext, mid, keys, hsend, onehot, even, odd, lever, hcat, msgs,
        facc, last, query, state, late, state_in, late_in, pos_in, aux, aux_in, chosen, aux_smem,
        radial, in_sem, aux_sem, send_sem, recv_sem,
    ) = refs
    rep = lax.axis_index("rep")
    dom = lax.axis_index("dom")
    has = (rep < reps - 1, rep > 0)
    dom_to = (lax.rem(dom + 1, doms), lax.rem(dom + doms - 1, doms))
    ladder = ((0, None, None), (1, has[0], has[1]), (-1, has[1], has[0]))

    def when(condition, action):
        if condition is None:
            action()
        else:
            pl.when(condition)(action)

    barrier = pltpu.get_barrier_semaphore()

    def greet(step, side):
        to = {"rep": rep + step} if side is None else {"rep": rep + step, "dom": dom_to[side]}
        pl.semaphore_signal(barrier, inc=1, device_id=to, device_id_type=MESH)

    for step, there, _ in ladder:
        for side in (0, 1) if step == 0 else (0, 1, None):
            when(there, lambda step=step, side=side: greet(step, side))

    loads = [
        pltpu.make_async_copy(ins[i], held[i], in_sem.at[i]) for i in range(17)
    ]
    for c in loads:
        c.start()

    def copy(number, to, src, dst):
        return pltpu.make_async_remote_copy(
            src_ref=src,
            dst_ref=dst,
            send_sem=send_sem.at[number],
            recv_sem=recv_sem.at[number],
            device_id=to,
            device_id_type=MESH,
        )

    for i in (8, 3, 0, 1, 2):
        loads[i].wait()
    kinds = kind_ref[...]
    mass = jnp.zeros((1, ATOMS), jnp.float32)
    for s in range(SPECIES):
        mass = jnp.where(kinds == s, inertia_ref[s], mass)
    inv_mass = 1.0 / mass
    moved, half = [], []
    for axis in range(3):
        loc, spd, frc = loc_ref[axis], spd_ref[axis], frc_ref[axis]
        moved.append(loc + time_step * spd + 0.5 * time_step * time_step * frc * inv_mass)
        half.append(spd + 0.5 * time_step * frc * inv_mass)
    kindf = kinds.astype(jnp.float32)
    for t in range(TILES):
        lanes = slice(t * TILE, (t + 1) * TILE)
        posext[t] = jnp.zeros((8, TILE), jnp.float32)
        for axis in range(3):
            posext[t, axis : axis + 1, :] = moved[axis][:, lanes]
        posext[t, 3:4, :] = kindf[:, lanes]

    loads[4].wait()
    first_row = lax.broadcasted_iota(jnp.int32, (8, TILE), 0) == 0
    for side in range(2):
        for g in range(GT):
            start = ((1 - side) * GT + g) * TILE
            label = jnp.broadcast_to(ghost_ref[:, start : start + TILE], (8, TILE))
            place = label & (TILE - 1)
            owner = label >> 7
            out = jnp.zeros((8, TILE), jnp.float32)
            for t in range(TILES):
                got = jnp.take_along_axis(posext[t], place, axis=1, mode="promise_in_bounds")
                out = jnp.where(owner == t, got, out)
            shift = slab_width if side == 1 else -slab_width
            psend[side, g] = jnp.where(first_row, out + shift, out)

    for axis in range(3):
        state[axis] = moved[axis]
        late[axis] = half[axis]
    state[3] = kindf
    late[3] = inv_mass
    late[4, :, 0 : 2 * GT * TILE] = ghost_ref[...].astype(jnp.float32)
    late[4, :, 2 * GT * TILE :] = jnp.zeros((1, ATOMS - 2 * GT * TILE), jnp.float32)
    loads[5].wait()
    loads[6].wait()
    aux[...] = jnp.zeros((8, TILE), jnp.int32)
    aux[0:NEI, 0:TILES] = adj_ref[0]
    aux[NEI : NEI + 1, 0:TILES] = live_ref[...]

    pl.semaphore_wait(barrier, 2 + 3 * (has[0].astype(jnp.int32) + has[1].astype(jnp.int32)))
    copies = []
    for n, (step, there, comes) in enumerate(ladder):
        for side in range(2):
            to = {"rep": rep + step, "dom": dom_to[side]}
            copies.append((copy(2 * n + side, to, psend.at[side], pos_in.at[n, side]), there, comes))
    for n, (step, there, comes) in enumerate(ladder[1:]):
        to = {"rep": rep + step}
        copies.append((copy(6 + n, to, state, state_in.at[n]), there, comes))
        copies.append((copy(8 + n, to, aux, aux_in.at[n]), there, comes))
    late_copies = [
        (copy(14 + n, {"rep": rep + step}, late, late_in.at[n]), there, comes)
        for n, (step, there, comes) in enumerate(ladder[1:])
    ]
    for c, there, _ in copies + late_copies:
        when(there, c.start)
    for n in (1, 2):

        @pl.when(jnp.logical_not(ladder[n][2]))
        def _():
            pos_in[n] = jnp.zeros((2, GT, 8, TILE), jnp.float32)
            state_in[n - 1] = jnp.zeros((4, 1, ATOMS), jnp.float32)
            late_in[n - 1] = jnp.zeros((5, 1, ATOMS), jnp.float32)
            aux_in[n - 1] = jnp.zeros((8, TILE), jnp.int32)

    for i in (7, 9, 10, 11, 12, 13, 14, 15, 16):
        loads[i].wait()
    lanef = lax.broadcasted_iota(jnp.int32, (TILE, TILE), 1).astype(jnp.float32)
    row = lax.broadcasted_iota(jnp.int32, (NB, CH), 0)
    scales = jnp.zeros((NB, CH), jnp.float32)
    for b in range(NB):
        scales = jnp.where(row == b, UNFOLD[b], scales)
    vectors = jnp.concatenate([vec_ref[...], jnp.zeros((TILE - SPECIES, CH), jnp.bfloat16)], axis=0)
    partner = swap_ref[rep]
    quotient = jnp.sqrt(
        jnp.full((1, ATOMS), heat_ref[rep], jnp.float32)
        / jnp.full((1, ATOMS), heat_ref[partner], jnp.float32)
    )
    for c, there, comes in copies:
        when(there, c.wait_send)
        when(comes, c.wait_recv)

    offset = jnp.full((8, TILE), partner - rep, jnp.int32)
    aux[...] = pick(offset, aux[...], aux_in[0], aux_in[1])
    to_smem = pltpu.make_async_copy(aux, aux_smem, aux_sem)
    to_smem.start()
    for side in range(2):
        for g in range(GT):
            posext[TILES + GT * side + g] = pick(
                offset, pos_in[0, side, g], pos_in[1, side, g], pos_in[2, side, g]
            )
    offset = jnp.full((1, ATOMS), partner - rep, jnp.int32)
    for row in range(4):
        chosen[row] = pick(offset, state[row], state_in[0, row], state_in[1, row])
    for t in range(TILES):
        lanes = slice(t * TILE, (t + 1) * TILE)
        for axis in range(3):
            posext[t, axis : axis + 1, :] = chosen[axis, :, lanes]
        posext[t, 3:4, :] = chosen[3, :, lanes]
    for s in range(EXT):
        posext[s, 4:7, :] = posext[s, 0:3, :] * SCALE
    for layer in range(2):
        radial[layer] = radial_ref[layer] * scales
    for axis in range(3):
        result[axis] = chosen[axis]

    def take_late():
        for c, there, comes in late_copies:
            when(there, c.wait_send)
            when(comes, c.wait_recv)
        for row in range(5):
            chosen[4 + row] = pick(offset, late[row], late_in[0, row], late_in[1, row])

    def embed(s):
        hot = jnp.where(columns(posext[s, 3:4, :]) == lanef, 1.0, 0.0).astype(jnp.bfloat16)
        hext[s] = jnp.dot(hot, vectors, preferred_element_type=jnp.float32).astype(jnp.bfloat16)

    def fill_onehot():
        for g in range(2 * GT):
            labels = columns(chosen[8, :, g * TILE : (g + 1) * TILE])
            for t in range(TILES):
                hot = jnp.where(labels == lanef + float(t * TILE), 1.0, 0.0).astype(jnp.bfloat16)
                onehot[t, g * TILE : (g + 1) * TILE, :] = hot

    to_smem.wait()

    def fill_basis(t, buffer, slot):
        for axis in range(3):
            xcol[t, axis] = columns(posext[t, 4 + axis : 5 + axis, :])
        for k in range(NEI):
            far = posext[aux_smem[k, t]]
            dead = jnp.clip(k + 1 - aux_smem[NEI, t], 0, 1).astype(jnp.float32) * FAR
            xj, yj, zj = far[4:5, :] + dead, far[5:6, :], far[6:7, :]
            for c in range(TILE // CHUNK):
                rows = slice(c * CHUNK, (c + 1) * CHUNK)
                dx = xj - xcol[t, 0, rows, :]
                dy = yj - xcol[t, 1, rows, :]
                dz = zj - xcol[t, 2, rows, :]
                square = dx * dx + dy * dy + dz * dz
                a = square * lax.rsqrt(jnp.maximum(square, 1e-30))
                top = a - TOP
                g = jnp.exp2(top * (TOP - a))
                q = jnp.exp2(a * (-2.0 * ROOT))
                for b in range(NB - 1, -1, -1):
                    buffer[slot, k, b, rows, :] = g.astype(jnp.bfloat16)
                    if b:
                        g = g * q

    def sum_messages(layer, t, buffer, slot, source, parity):
        for k in range(NEI):
            hcat[parity, k * TILE : (k + 1) * TILE, :] = source[aux_smem[k, t]]
        parts = []
        for k in range(0, NEI, 2):
            flat = jnp.concatenate(
                [buffer[slot, k + i].reshape(NB * TILE, TILE) for i in range(2)], axis=1
            )
            parts.append(
                jnp.dot(
                    flat,
                    hcat[parity, k * TILE : (k + 2) * TILE, :],
                    preferred_element_type=jnp.float32,
                )
            )
        summed = parts[0] + parts[1]
        weights = radial[layer]
        messages = weights[0:1, :] * summed[0:TILE, :]
        for b in range(1, NB):
            messages = messages + weights[b : b + 1, :] * summed[b * TILE : (b + 1) * TILE, :]
        msgs[parity] = messages

    def refresh(layer, t, source, parity):
        messages = msgs[parity]
        inverse = lax.rsqrt(jnp.mean(messages * messages, axis=-1, keepdims=True) + norm_eps)
        scaled = messages * inverse * gain_ref[layer : layer + 1, :]
        activation = (scaled / (1.0 + jnp.exp(-scaled))).astype(jnp.bfloat16)
        return (
            source[t].astype(jnp.float32)
            + jnp.dot(activation, mix_ref[layer], preferred_element_type=jnp.float32)
        ).astype(jnp.bfloat16)

    halves = (even, odd)

    def fill(t, u, parity):
        fill_basis(t, halves[parity], u)

    def run_layer(layer, source, finish, prepare):
        def gather(t, u, parity):
            sum_messages(layer, t, halves[parity], u, source, parity)

        def end(t, parity):
            finish(t, refresh(layer, t, source, parity))

        if prepare:
            fill(1, 0, 1)
        gather(0, 0, 0)

        def pair(u, _):
            if prepare:
                fill(2 * u + 2, u + 1, 0)
            gather(2 * u + 1, u, 1)
            end(2 * u, 0)
            if prepare:
                fill(2 * u + 3, u + 1, 1)
            gather(2 * u + 2, u + 1, 0)
            end(2 * u + 1, 1)
            return 0

        lax.fori_loop(0, TILES // 2 - 1, pair, 0)
        if prepare:
            take_late()
            fill_onehot()
        gather(TILES - 1, TILES // 2 - 1, 1)
        end(TILES - 2, 0)
        end(TILES - 1, 1)

    fill(0, 0, 0)
    for s in range(EXT):
        embed(s)

    def keep_mid(t, hidden):
        mid[t] = hidden

    run_layer(0, hext, keep_mid, True)

    first = 1 - jnp.minimum(lax.rem(dom, doms // 2), 1)

    def export(stage, rows, buffer, slot):
        copies = []
        for turn in range(2):
            side = lax.rem(first + turn, 2)
            start = pl.multiple_of((1 - side) * GT * TILE, GT * TILE)
            hot = jnp.concatenate(
                [onehot[t, pl.ds(start, GT * TILE), :] for t in range(TILES)], axis=1
            )
            packed = jnp.dot(hot, rows, preferred_element_type=jnp.float32)
            hsend[slot, turn] = packed.astype(jnp.bfloat16).reshape(GT, TILE, CH)
            c = copy(
                2 * stage + side,
                {"dom": lax.rem(dom + 1 - 2 * side + doms, doms)},
                hsend.at[slot, turn],
                buffer.at[pl.ds(TILES + GT * side, GT)],
            )
            c.start()
            copies.append(c)
        return copies

    mid_copies = export(5, mid[0:TILES].reshape(ATOMS, CH), mid, 0)

    taper = [taper_ref[b] * (UNFOLD[b] * factor / SCALE) for b in range(NB)]

    def fill_lever(u, _):
        for parity in range(2):
            t = 2 * u + parity
            for k in range(NEI):
                far = posext[aux_smem[k, t]]
                for c in range(TILE // CHUNK):
                    rows = slice(c * CHUNK, (c + 1) * CHUNK)
                    total = taper[0] * halves[parity][u, k, 0, rows, :].astype(jnp.float32)
                    for b in range(1, NB):
                        total = total + taper[b] * halves[parity][u, k, b, rows, :].astype(
                            jnp.float32
                        )
                    for axis in range(3):
                        lever[t, k, axis, rows, :] = total * (
                            far[4 + axis : 5 + axis, :] - xcol[t, axis, rows, :]
                        )
        return 0

    lax.fori_loop(0, TILES // 2, fill_lever, 0)

    for c in mid_copies:
        c.wait()

    def keep_last(t, hidden):
        last[t] = hidden
        keys[t] = jnp.dot(
            hidden, source_ref[...], preferred_element_type=jnp.float32
        ).astype(jnp.bfloat16)

    run_layer(1, mid, keep_last, False)
    key_copies = export(6, keys[0:TILES].reshape(ATOMS, CH), keys, 1)

    query[...] = (
        jnp.dot(
            last[...].reshape(ATOMS, CH), target_ref[...], preferred_element_type=jnp.float32
        )
        .astype(jnp.bfloat16)
        .reshape(TILES, TILE, CH)
    )
    for c in key_copies:
        c.wait()

    def force_pair(u, _):
        for parity in range(2):
            t = 2 * u + parity
            for k in range(NEI):
                hcat[parity, k * TILE : (k + 1) * TILE, :] = keys[aux_smem[k, t]]
            scores = lax.dot_general(
                query[t],
                hcat[parity],
                (((1,), (1,)), ((), ())),
                preferred_element_type=jnp.float32,
            )
            for axis in range(3):
                total = scores[:, 0:TILE] * lever[t, 0, axis]
                for k in range(1, NEI):
                    total = total + scores[:, k * TILE : (k + 1) * TILE] * lever[t, k, axis]
                facc[parity, axis] = total
            lanes = pl.ds(pl.multiple_of(t * TILE, TILE), TILE)
            for axis in range(3):
                result[6 + axis, :, lanes] = jnp.sum(facc[parity, axis].T, axis=0, keepdims=True)
        return 0

    lax.fori_loop(0, TILES // 2, force_pair, 0)

    for axis in range(3):
        force = result[6 + axis]
        result[3 + axis] = (chosen[4 + axis] + 0.5 * time_step * force * chosen[7]) * quotient


def hand_out(packed, pos_out, vel_out, frc_out, sem):
    copies = [
        pltpu.make_async_copy(packed.at[pl.ds(3 * i, 3)], ref, sem.at[i])
        for i, ref in enumerate((pos_out, vel_out, frc_out))
    ]
    for c in copies:
        c.start()
    for c in copies:
        c.wait()


def solution(mesh):
    reps, doms = mesh.shape["rep"], mesh.shape["dom"]

    def kernel(*refs):
        step_kernel(reps, doms, *refs)

    def local(*args):
        args = list(args)
        for i in range(3):
            args[i] = jnp.transpose(args[i], (1, 0, 2))
        args[5] = jnp.transpose(args[5], (0, 2, 1))
        vmem = pl.BlockSpec(memory_space=pltpu.VMEM)
        hbm = pl.BlockSpec(memory_space=pltpu.HBM)
        out = jax.ShapeDtypeStruct((3, 1, ATOMS), jnp.float32)
        f32, bf16 = jnp.float32, jnp.bfloat16
        scalar = (8, 14, 15, 16)
        held = [
            (pltpu.SMEM if i in scalar else pltpu.VMEM)(x.shape, x.dtype)
            for i, x in enumerate(args)
        ]
        packed = pl.pallas_call(
            kernel,
            out_shape=jax.ShapeDtypeStruct((9, 1, ATOMS), jnp.float32),
            in_specs=[hbm] * 17,
            out_specs=vmem,
            scratch_shapes=held
            + [
                pltpu.VMEM((EXT, 8, TILE), f32),
                pltpu.VMEM((2, GT, 8, TILE), f32),
                pltpu.VMEM((TILES, 3, TILE, TILE), f32),
                pltpu.VMEM((EXT, TILE, CH), bf16),
                pltpu.VMEM((EXT, TILE, CH), bf16),
                pltpu.VMEM((EXT, TILE, CH), bf16),
                pltpu.VMEM((2, 2, GT, TILE, CH), bf16),
                pltpu.VMEM((TILES, 2 * GT * TILE, TILE), bf16),
                pltpu.VMEM((TILES // 2, NEI, NB, TILE, TILE), bf16),
                pltpu.VMEM((TILES // 2, NEI, NB, TILE, TILE), bf16),
                pltpu.VMEM((TILES, NEI, 3, TILE, TILE), f32),
                pltpu.VMEM((2, NEI * TILE, CH), bf16),
                pltpu.VMEM((2, TILE, CH), f32),
                pltpu.VMEM((2, 3, TILE, TILE), f32),
                pltpu.VMEM((TILES, TILE, CH), bf16),
                pltpu.VMEM((TILES, TILE, CH), bf16),
                pltpu.VMEM((4, 1, ATOMS), f32),
                pltpu.VMEM((5, 1, ATOMS), f32),
                pltpu.VMEM((2, 4, 1, ATOMS), f32),
                pltpu.VMEM((2, 5, 1, ATOMS), f32),
                pltpu.VMEM((3, 2, GT, 8, TILE), f32),
                pltpu.VMEM((8, TILE), jnp.int32),
                pltpu.VMEM((2, 8, TILE), jnp.int32),
                pltpu.VMEM((9, 1, ATOMS), f32),
                pltpu.SMEM((8, TILE), jnp.int32),
                pltpu.VMEM((2, NB, CH), f32),
                pltpu.SemaphoreType.DMA((17,)),
                pltpu.SemaphoreType.DMA,
                pltpu.SemaphoreType.DMA((16,)),
                pltpu.SemaphoreType.DMA((16,)),
            ],
            compiler_params=pltpu.CompilerParams(
                collective_id=0, has_side_effects=True, vmem_limit_bytes=66850000
            ),
            name="md_step",
        )(*args)
        outs = pl.pallas_call(
            hand_out,
            out_shape=(out, out, out),
            in_specs=[vmem],
            out_specs=(hbm, hbm, hbm),
            scratch_shapes=[pltpu.SemaphoreType.DMA((3,))],
            compiler_params=pltpu.CompilerParams(vmem_limit_bytes=1048576),
            name="hand_out",
        )(packed)
        return tuple(jnp.transpose(x, (1, 0, 2)) for x in outs)

    in_specs = (
        P("rep", None, "dom"),
        P("rep", None, "dom"),
        P("rep", None, "dom"),
        P("rep", "dom"),
        P("rep", "dom"),
        P("rep", "dom", None),
        P("rep", "dom"),
        P(), P(), P(), P(), P(), P(), P(), P(), P(), P(),
    )
    out_specs = (P("rep", None, "dom"), P("rep", None, "dom"), P("rep", None, "dom"))
    return jax.shard_map(local, mesh=mesh, in_specs=in_specs, out_specs=out_specs, check_vma=False)
```

```python
import math

import jax
import jax.numpy as jnp
from jax import lax
from jax.experimental import pallas as pl
from jax.experimental.pallas import tpu as pltpu
from jax.sharding import PartitionSpec as P

NB = 8
TILE = 128
NEI = 4
TILES = 8
GT = 3
EXT = TILES + 2 * GT
ATOMS = TILES * TILE
SPECIES = 16
CH = 128
CHUNK = 32

slab_width = 1.5
time_step = 0.5
basis_width = 0.3
norm_eps = 1e-06
factor = 1.0 / math.sqrt(CH * NEI * TILE)

ROOT = math.sqrt(math.log2(math.e))
SCALE = ROOT / basis_width
TOP = (NB - 1) * ROOT
FAR = 1.0e3
UNFOLD = [math.exp((NB - 1) ** 2 - b * b) for b in range(NB)]

MESH = pl.DeviceIdType.MESH


def columns(row):
    return jnp.broadcast_to(row, (TILE, TILE)).T


def pick(offset, own, low, high):
    return jnp.where(offset == 1, high, jnp.where(offset == -1, low, own))


def step_kernel(reps, doms, *refs):
    ins, refs = refs[:17], refs[17:]
    (result,), refs = refs[:1], refs[1:]
    held, refs = refs[:17], refs[17:]
    (
        loc_ref, spd_ref, frc_ref, kind_ref, ghost_ref, adj_ref, live_ref, vec_ref, inertia_ref,
        radial_ref, gain_ref, mix_ref, target_ref, source_ref, taper_ref, heat_ref, swap_ref,
    ) = held
    (
        posext, psend, xcol, hext, mid, hsend, onehot, even, odd, lever, hcat, msgs,
        facc, last, query, state, late, state_in, late_in, pos_in, aux, aux_in, chosen, aux_smem,
        radial, in_sem, aux_sem, send_sem, recv_sem,
    ) = refs
    rep = lax.axis_index("rep")
    dom = lax.axis_index("dom")
    has = (rep < reps - 1, rep > 0)
    dom_to = (lax.rem(dom + 1, doms), lax.rem(dom + doms - 1, doms))
    ladder = ((0, None, None), (1, has[0], has[1]), (-1, has[1], has[0]))

    def when(condition, action):
        if condition is None:
            action()
        else:
            pl.when(condition)(action)

    barrier = pltpu.get_barrier_semaphore()

    def greet(step, side):
        to = {"rep": rep + step} if side is None else {"rep": rep + step, "dom": dom_to[side]}
        pl.semaphore_signal(barrier, inc=1, device_id=to, device_id_type=MESH)

    for step, there, _ in ladder:
        for side in (0, 1) if step == 0 else (0, 1, None):
            when(there, lambda step=step, side=side: greet(step, side))

    loads = [
        pltpu.make_async_copy(ins[i], held[i], in_sem.at[i]) for i in range(17)
    ]
    for c in loads:
        c.start()

    def copy(number, to, src, dst):
        return pltpu.make_async_remote_copy(
            src_ref=src,
            dst_ref=dst,
            send_sem=send_sem.at[number],
            recv_sem=recv_sem.at[number],
            device_id=to,
            device_id_type=MESH,
        )

    for i in (8, 3, 0, 1, 2):
        loads[i].wait()
    kinds = kind_ref[...]
    mass = jnp.zeros((1, ATOMS), jnp.float32)
    for s in range(SPECIES):
        mass = jnp.where(kinds == s, inertia_ref[s], mass)
    inv_mass = 1.0 / mass
    moved, half = [], []
    for axis in range(3):
        loc, spd, frc = loc_ref[axis], spd_ref[axis], frc_ref[axis]
        moved.append(loc + time_step * spd + 0.5 * time_step * time_step * frc * inv_mass)
        half.append(spd + 0.5 * time_step * frc * inv_mass)
    kindf = kinds.astype(jnp.float32)
    for t in range(TILES):
        lanes = slice(t * TILE, (t + 1) * TILE)
        posext[t] = jnp.zeros((8, TILE), jnp.float32)
        for axis in range(3):
            posext[t, axis : axis + 1, :] = moved[axis][:, lanes]
        posext[t, 3:4, :] = kindf[:, lanes]

    loads[4].wait()
    first_row = lax.broadcasted_iota(jnp.int32, (8, TILE), 0) == 0
    for side in range(2):
        for g in range(GT):
            start = ((1 - side) * GT + g) * TILE
            label = jnp.broadcast_to(ghost_ref[:, start : start + TILE], (8, TILE))
            place = label & (TILE - 1)
            owner = label >> 7
            out = jnp.zeros((8, TILE), jnp.float32)
            for t in range(TILES):
                got = jnp.take_along_axis(posext[t], place, axis=1, mode="promise_in_bounds")
                out = jnp.where(owner == t, got, out)
            shift = slab_width if side == 1 else -slab_width
            psend[side, g] = jnp.where(first_row, out + shift, out)

    for axis in range(3):
        state[axis] = moved[axis]
        late[axis] = half[axis]
    state[3] = kindf
    late[3] = inv_mass
    late[4, :, 0 : 2 * GT * TILE] = ghost_ref[...].astype(jnp.float32)
    late[4, :, 2 * GT * TILE :] = jnp.zeros((1, ATOMS - 2 * GT * TILE), jnp.float32)
    loads[5].wait()
    loads[6].wait()
    aux[...] = jnp.zeros((8, TILE), jnp.int32)
    aux[0:NEI, 0:TILES] = adj_ref[0]
    aux[NEI : NEI + 1, 0:TILES] = live_ref[...]

    pl.semaphore_wait(barrier, 2 + 3 * (has[0].astype(jnp.int32) + has[1].astype(jnp.int32)))
    copies = []
    for n, (step, there, comes) in enumerate(ladder):
        for side in range(2):
            to = {"rep": rep + step, "dom": dom_to[side]}
            copies.append((copy(2 * n + side, to, psend.at[side], pos_in.at[n, side]), there, comes))
    for n, (step, there, comes) in enumerate(ladder[1:]):
        to = {"rep": rep + step}
        copies.append((copy(6 + n, to, state, state_in.at[n]), there, comes))
        copies.append((copy(8 + n, to, aux, aux_in.at[n]), there, comes))
    late_copies = [
        (copy(14 + n, {"rep": rep + step}, late, late_in.at[n]), there, comes)
        for n, (step, there, comes) in enumerate(ladder[1:])
    ]
    for c, there, _ in copies + late_copies:
        when(there, c.start)
    for n in (1, 2):

        @pl.when(jnp.logical_not(ladder[n][2]))
        def _():
            pos_in[n] = jnp.zeros((2, GT, 8, TILE), jnp.float32)
            state_in[n - 1] = jnp.zeros((4, 1, ATOMS), jnp.float32)
            late_in[n - 1] = jnp.zeros((5, 1, ATOMS), jnp.float32)
            aux_in[n - 1] = jnp.zeros((8, TILE), jnp.int32)

    for i in (7, 9, 10, 11, 12, 13, 14, 15, 16):
        loads[i].wait()
    lanef = lax.broadcasted_iota(jnp.int32, (TILE, TILE), 1).astype(jnp.float32)
    row = lax.broadcasted_iota(jnp.int32, (NB, CH), 0)
    scales = jnp.zeros((NB, CH), jnp.float32)
    for b in range(NB):
        scales = jnp.where(row == b, UNFOLD[b], scales)
    vectors = jnp.concatenate([vec_ref[...], jnp.zeros((TILE - SPECIES, CH), jnp.bfloat16)], axis=0)
    partner = swap_ref[rep]
    quotient = jnp.sqrt(
        jnp.full((1, ATOMS), heat_ref[rep], jnp.float32)
        / jnp.full((1, ATOMS), heat_ref[partner], jnp.float32)
    )
    for c, there, comes in copies:
        when(there, c.wait_send)
        when(comes, c.wait_recv)

    offset = jnp.full((8, TILE), partner - rep, jnp.int32)
    aux[...] = pick(offset, aux[...], aux_in[0], aux_in[1])
    to_smem = pltpu.make_async_copy(aux, aux_smem, aux_sem)
    to_smem.start()
    for side in range(2):
        for g in range(GT):
            posext[TILES + GT * side + g] = pick(
                offset, pos_in[0, side, g], pos_in[1, side, g], pos_in[2, side, g]
            )
    offset = jnp.full((1, ATOMS), partner - rep, jnp.int32)
    for row in range(4):
        chosen[row] = pick(offset, state[row], state_in[0, row], state_in[1, row])
    for t in range(TILES):
        lanes = slice(t * TILE, (t + 1) * TILE)
        for axis in range(3):
            posext[t, axis : axis + 1, :] = chosen[axis, :, lanes]
        posext[t, 3:4, :] = chosen[3, :, lanes]
    for s in range(EXT):
        posext[s, 4:7, :] = posext[s, 0:3, :] * SCALE
    for layer in range(2):
        radial[layer] = radial_ref[layer] * scales
    for axis in range(3):
        result[axis] = chosen[axis]

    def take_late():
        for c, there, comes in late_copies:
            when(there, c.wait_send)
            when(comes, c.wait_recv)
        for row in range(5):
            chosen[4 + row] = pick(offset, late[row], late_in[0, row], late_in[1, row])

    def embed(s):
        hot = jnp.where(columns(posext[s, 3:4, :]) == lanef, 1.0, 0.0).astype(jnp.bfloat16)
        hext[s] = jnp.dot(hot, vectors, preferred_element_type=jnp.float32).astype(jnp.bfloat16)

    def fill_onehot():
        for g in range(2 * GT):
            labels = columns(chosen[8, :, g * TILE : (g + 1) * TILE])
            for t in range(TILES):
                hot = jnp.where(labels == lanef + float(t * TILE), 1.0, 0.0).astype(jnp.bfloat16)
                onehot[t, g * TILE : (g + 1) * TILE, :] = hot

    to_smem.wait()

    def fill_basis(t, buffer, slot):
        for axis in range(3):
            xcol[t, axis] = columns(posext[t, 4 + axis : 5 + axis, :])
        for k in range(NEI):
            far = posext[aux_smem[k, t]]
            dead = jnp.clip(k + 1 - aux_smem[NEI, t], 0, 1).astype(jnp.float32) * FAR
            xj, yj, zj = far[4:5, :] + dead, far[5:6, :], far[6:7, :]
            for c in range(TILE // CHUNK):
                rows = slice(c * CHUNK, (c + 1) * CHUNK)
                dx = xj - xcol[t, 0, rows, :]
                dy = yj - xcol[t, 1, rows, :]
                dz = zj - xcol[t, 2, rows, :]
                square = dx * dx + dy * dy + dz * dz
                a = square * lax.rsqrt(jnp.maximum(square, 1e-30))
                top = a - TOP
                g = jnp.exp2(top * (TOP - a))
                q = jnp.exp2(a * (-2.0 * ROOT))
                for b in range(NB - 1, -1, -1):
                    buffer[slot, k, b, rows, :] = g.astype(jnp.bfloat16)
                    if b:
                        g = g * q

    def sum_messages(layer, t, buffer, slot, source, parity):
        for k in range(NEI):
            hcat[parity, k * TILE : (k + 1) * TILE, :] = source[aux_smem[k, t]]
        parts = []
        for k in range(0, NEI, 2):
            flat = jnp.concatenate(
                [buffer[slot, k + i].reshape(NB * TILE, TILE) for i in range(2)], axis=1
            )
            parts.append(
                jnp.dot(
                    flat,
                    hcat[parity, k * TILE : (k + 2) * TILE, :],
                    preferred_element_type=jnp.float32,
                )
            )
        summed = parts[0] + parts[1]
        weights = radial[layer]
        messages = weights[0:1, :] * summed[0:TILE, :]
        for b in range(1, NB):
            messages = messages + weights[b : b + 1, :] * summed[b * TILE : (b + 1) * TILE, :]
        msgs[parity] = messages

    def refresh(layer, t, source, parity):
        messages = msgs[parity]
        inverse = lax.rsqrt(jnp.mean(messages * messages, axis=-1, keepdims=True) + norm_eps)
        scaled = messages * inverse * gain_ref[layer : layer + 1, :]
        activation = (scaled / (1.0 + jnp.exp(-scaled))).astype(jnp.bfloat16)
        return (
            source[t].astype(jnp.float32)
            + jnp.dot(activation, mix_ref[layer], preferred_element_type=jnp.float32)
        ).astype(jnp.bfloat16)

    halves = (even, odd)

    def fill(t, u, parity):
        fill_basis(t, halves[parity], u)

    def run_layer(layer, source, finish, prepare):
        def gather(t, u, parity):
            sum_messages(layer, t, halves[parity], u, source, parity)

        def end(t, parity):
            finish(t, refresh(layer, t, source, parity))

        if prepare:
            fill(1, 0, 1)
        gather(0, 0, 0)

        def pair(u, _):
            if prepare:
                fill(2 * u + 2, u + 1, 0)
            gather(2 * u + 1, u, 1)
            end(2 * u, 0)
            if prepare:
                fill(2 * u + 3, u + 1, 1)
            gather(2 * u + 2, u + 1, 0)
            end(2 * u + 1, 1)
            return 0

        lax.fori_loop(0, TILES // 2 - 1, pair, 0)
        if prepare:
            take_late()
            fill_onehot()
        gather(TILES - 1, TILES // 2 - 1, 1)
        end(TILES - 2, 0)
        end(TILES - 1, 1)

    fill(0, 0, 0)
    for s in range(EXT):
        embed(s)

    def keep_mid(t, hidden):
        mid[t] = hidden

    run_layer(0, hext, keep_mid, True)

    first = 1 - jnp.minimum(lax.rem(dom, doms // 2), 1)

    def export(stage, rows, buffer, slot):
        copies = []
        for turn in range(2):
            side = lax.rem(first + turn, 2)
            to = {"dom": lax.rem(dom + 1 - 2 * side + doms, doms)}
            for g in range(GT):
                start = pl.multiple_of(((1 - side) * GT + g) * TILE, TILE)
                hot = jnp.concatenate(
                    [onehot[t, pl.ds(start, TILE), :] for t in range(TILES)], axis=1
                )
                packed = jnp.dot(hot, rows, preferred_element_type=jnp.float32)
                hsend[slot, turn, g] = packed.astype(jnp.bfloat16)
                c = copy(
                    2 * GT * stage + GT * side + g,
                    to,
                    hsend.at[slot, turn, g],
                    buffer.at[TILES + GT * side + g],
                )
                c.start()
                copies.append(c)
        return copies

    mid_copies = export(3, mid[0:TILES].reshape(ATOMS, CH), mid, 0)

    taper = [taper_ref[b] * (UNFOLD[b] * factor / SCALE) for b in range(NB)]

    def fill_lever(u, _):
        for parity in range(2):
            t = 2 * u + parity
            for k in range(NEI):
                far = posext[aux_smem[k, t]]
                for c in range(TILE // CHUNK):
                    rows = slice(c * CHUNK, (c + 1) * CHUNK)
                    total = taper[0] * halves[parity][u, k, 0, rows, :].astype(jnp.float32)
                    for b in range(1, NB):
                        total = total + taper[b] * halves[parity][u, k, b, rows, :].astype(
                            jnp.float32
                        )
                    for axis in range(3):
                        lever[t, k, axis, rows, :] = total * (
                            far[4 + axis : 5 + axis, :] - xcol[t, axis, rows, :]
                        )
        return 0

    lax.fori_loop(0, TILES // 2, fill_lever, 0)

    for c in mid_copies:
        c.wait()

    def keep_last(t, hidden):
        last[t] = hidden

    run_layer(1, mid, keep_last, False)
    key_copies = export(4, last[0:TILES].reshape(ATOMS, CH), last, 1)

    rows = last[0:TILES].reshape(ATOMS, CH)
    asked = jnp.dot(rows, target_ref[...], preferred_element_type=jnp.float32).astype(jnp.bfloat16)
    asked = lax.dot_general(
        asked, source_ref[...], (((1,), (1,)), ((), ())), preferred_element_type=jnp.float32
    )
    query[...] = asked.astype(jnp.bfloat16).reshape(TILES, TILE, CH)

    for c in key_copies:
        c.wait()

    def force_pair(u, _):
        for parity in range(2):
            t = 2 * u + parity
            for k in range(NEI):
                hcat[parity, k * TILE : (k + 1) * TILE, :] = last[aux_smem[k, t]]
            scores = lax.dot_general(
                query[t],
                hcat[parity],
                (((1,), (1,)), ((), ())),
                preferred_element_type=jnp.float32,
            )
            for axis in range(3):
                total = scores[:, 0:TILE] * lever[t, 0, axis]
                for k in range(1, NEI):
                    total = total + scores[:, k * TILE : (k + 1) * TILE] * lever[t, k, axis]
                facc[parity, axis] = total
            lanes = pl.ds(pl.multiple_of(t * TILE, TILE), TILE)
            for axis in range(3):
                result[6 + axis, :, lanes] = jnp.sum(facc[parity, axis].T, axis=0, keepdims=True)
        return 0

    lax.fori_loop(0, TILES // 2, force_pair, 0)

    for axis in range(3):
        force = result[6 + axis]
        result[3 + axis] = (chosen[4 + axis] + 0.5 * time_step * force * chosen[7]) * quotient


def hand_out(packed, pos_out, vel_out, frc_out, sem):
    copies = [
        pltpu.make_async_copy(packed.at[pl.ds(3 * i, 3)], ref, sem.at[i])
        for i, ref in enumerate((pos_out, vel_out, frc_out))
    ]
    for c in copies:
        c.start()
    for c in copies:
        c.wait()


def solution(mesh):
    reps, doms = mesh.shape["rep"], mesh.shape["dom"]

    def kernel(*refs):
        step_kernel(reps, doms, *refs)

    def local(*args):
        args = list(args)
        for i in range(3):
            args[i] = jnp.transpose(args[i], (1, 0, 2))
        args[5] = jnp.transpose(args[5], (0, 2, 1))
        vmem = pl.BlockSpec(memory_space=pltpu.VMEM)
        hbm = pl.BlockSpec(memory_space=pltpu.HBM)
        out = jax.ShapeDtypeStruct((3, 1, ATOMS), jnp.float32)
        f32, bf16 = jnp.float32, jnp.bfloat16
        scalar = (8, 14, 15, 16)
        held = [
            (pltpu.SMEM if i in scalar else pltpu.VMEM)(x.shape, x.dtype)
            for i, x in enumerate(args)
        ]
        packed = pl.pallas_call(
            kernel,
            out_shape=jax.ShapeDtypeStruct((9, 1, ATOMS), jnp.float32),
            in_specs=[hbm] * 17,
            out_specs=vmem,
            scratch_shapes=held
            + [
                pltpu.VMEM((EXT, 8, TILE), f32),
                pltpu.VMEM((2, GT, 8, TILE), f32),
                pltpu.VMEM((TILES, 3, TILE, TILE), f32),
                pltpu.VMEM((EXT, TILE, CH), bf16),
                pltpu.VMEM((EXT, TILE, CH), bf16),
                pltpu.VMEM((2, 2, GT, TILE, CH), bf16),
                pltpu.VMEM((TILES, 2 * GT * TILE, TILE), bf16),
                pltpu.VMEM((TILES // 2, NEI, NB, TILE, TILE), bf16),
                pltpu.VMEM((TILES // 2, NEI, NB, TILE, TILE), bf16),
                pltpu.VMEM((TILES, NEI, 3, TILE, TILE), f32),
                pltpu.VMEM((2, NEI * TILE, CH), bf16),
                pltpu.VMEM((2, TILE, CH), f32),
                pltpu.VMEM((2, 3, TILE, TILE), f32),
                pltpu.VMEM((EXT, TILE, CH), bf16),
                pltpu.VMEM((TILES, TILE, CH), bf16),
                pltpu.VMEM((4, 1, ATOMS), f32),
                pltpu.VMEM((5, 1, ATOMS), f32),
                pltpu.VMEM((2, 4, 1, ATOMS), f32),
                pltpu.VMEM((2, 5, 1, ATOMS), f32),
                pltpu.VMEM((3, 2, GT, 8, TILE), f32),
                pltpu.VMEM((8, TILE), jnp.int32),
                pltpu.VMEM((2, 8, TILE), jnp.int32),
                pltpu.VMEM((9, 1, ATOMS), f32),
                pltpu.SMEM((8, TILE), jnp.int32),
                pltpu.VMEM((2, NB, CH), f32),
                pltpu.SemaphoreType.DMA((17,)),
                pltpu.SemaphoreType.DMA,
                pltpu.SemaphoreType.DMA((30,)),
                pltpu.SemaphoreType.DMA((30,)),
            ],
            compiler_params=pltpu.CompilerParams(
                collective_id=0, has_side_effects=True, vmem_limit_bytes=66850000
            ),
            name="md_step",
        )(*args)
        outs = pl.pallas_call(
            hand_out,
            out_shape=(out, out, out),
            in_specs=[vmem],
            out_specs=(hbm, hbm, hbm),
            scratch_shapes=[pltpu.SemaphoreType.DMA((3,))],
            compiler_params=pltpu.CompilerParams(vmem_limit_bytes=1048576),
            name="hand_out",
        )(packed)
        return tuple(jnp.transpose(x, (1, 0, 2)) for x in outs)

    in_specs = (
        P("rep", None, "dom"),
        P("rep", None, "dom"),
        P("rep", None, "dom"),
        P("rep", "dom"),
        P("rep", "dom"),
        P("rep", "dom", None),
        P("rep", "dom"),
        P(), P(), P(), P(), P(), P(), P(), P(), P(), P(),
    )
    out_specs = (P("rep", None, "dom"), P("rep", None, "dom"), P("rep", None, "dom"))
    return jax.shard_map(local, mesh=mesh, in_specs=in_specs, out_specs=out_specs, check_vma=False)
```

```python
import math

import jax
import jax.numpy as jnp
from jax import lax
from jax.experimental import pallas as pl
from jax.experimental.pallas import tpu as pltpu
from jax.sharding import PartitionSpec as P

NB = 8
TILE = 128
NEI = 4
TILES = 8
GT = 3
EXT = TILES + 2 * GT
ATOMS = TILES * TILE
SPECIES = 16
CH = 128
CHUNK = 32

slab_width = 1.5
time_step = 0.5
basis_width = 0.3
norm_eps = 1e-06
factor = 1.0 / math.sqrt(CH * NEI * TILE)

ROOT = math.sqrt(math.log2(math.e))
SCALE = ROOT / basis_width
TOP = (NB - 1) * ROOT
FAR = 1.0e3
UNFOLD = [math.exp((NB - 1) ** 2 - b * b) for b in range(NB)]

MESH = pl.DeviceIdType.MESH


def columns(row):
    return jnp.broadcast_to(row, (TILE, TILE)).T


def pick(offset, own, low, high):
    return jnp.where(offset == 1, high, jnp.where(offset == -1, low, own))


def step_kernel(reps, doms, *refs):
    ins, refs = refs[:17], refs[17:]
    (result,), refs = refs[:1], refs[1:]
    held, refs = refs[:17], refs[17:]
    (
        loc_ref, spd_ref, frc_ref, kind_ref, ghost_ref, adj_ref, live_ref, vec_ref, inertia_ref,
        radial_ref, gain_ref, mix_ref, target_ref, source_ref, taper_ref, heat_ref, swap_ref,
    ) = held
    (
        posext, psend, xcol, hext, mid, hsend, onehot, even, odd, lever, hcat, msgs,
        facc, last, query, state, late, state_in, late_in, pos_in, aux, aux_in, chosen, aux_smem,
        radial, in_sem, aux_sem, send_sem, recv_sem,
    ) = refs
    rep = lax.axis_index("rep")
    dom = lax.axis_index("dom")
    has = (rep < reps - 1, rep > 0)
    dom_to = (lax.rem(dom + 1, doms), lax.rem(dom + doms - 1, doms))
    ladder = ((0, None, None), (1, has[0], has[1]), (-1, has[1], has[0]))

    def when(condition, action):
        if condition is None:
            action()
        else:
            pl.when(condition)(action)

    barrier = pltpu.get_barrier_semaphore()

    def greet(step, side):
        to = {"rep": rep + step} if side is None else {"rep": rep + step, "dom": dom_to[side]}
        pl.semaphore_signal(barrier, inc=1, device_id=to, device_id_type=MESH)

    for step, there, _ in ladder:
        for side in (0, 1) if step == 0 else (0, 1, None):
            when(there, lambda step=step, side=side: greet(step, side))

    loads = [
        pltpu.make_async_copy(ins[i], held[i], in_sem.at[i]) for i in range(17)
    ]
    for c in loads:
        c.start()

    def copy(number, to, src, dst):
        return pltpu.make_async_remote_copy(
            src_ref=src,
            dst_ref=dst,
            send_sem=send_sem.at[number],
            recv_sem=recv_sem.at[number],
            device_id=to,
            device_id_type=MESH,
        )

    for i in (8, 3, 0, 1, 2):
        loads[i].wait()
    kinds = kind_ref[...]
    mass = jnp.zeros((1, ATOMS), jnp.float32)
    for s in range(SPECIES):
        mass = jnp.where(kinds == s, inertia_ref[s], mass)
    inv_mass = 1.0 / mass
    moved, half = [], []
    for axis in range(3):
        loc, spd, frc = loc_ref[axis], spd_ref[axis], frc_ref[axis]
        moved.append(loc + time_step * spd + 0.5 * time_step * time_step * frc * inv_mass)
        half.append(spd + 0.5 * time_step * frc * inv_mass)
    kindf = kinds.astype(jnp.float32)
    for t in range(TILES):
        lanes = slice(t * TILE, (t + 1) * TILE)
        posext[t] = jnp.zeros((8, TILE), jnp.float32)
        for axis in range(3):
            posext[t, axis : axis + 1, :] = moved[axis][:, lanes]
        posext[t, 3:4, :] = kindf[:, lanes]

    loads[4].wait()
    first_row = lax.broadcasted_iota(jnp.int32, (8, TILE), 0) == 0
    for side in range(2):
        for g in range(GT):
            start = ((1 - side) * GT + g) * TILE
            label = jnp.broadcast_to(ghost_ref[:, start : start + TILE], (8, TILE))
            place = label & (TILE - 1)
            owner = label >> 7
            out = jnp.zeros((8, TILE), jnp.float32)
            for t in range(TILES):
                got = jnp.take_along_axis(posext[t], place, axis=1, mode="promise_in_bounds")
                out = jnp.where(owner == t, got, out)
            shift = slab_width if side == 1 else -slab_width
            psend[side, g] = jnp.where(first_row, out + shift, out)

    for axis in range(3):
        state[axis] = moved[axis]
        late[axis] = half[axis]
    state[3] = kindf
    late[3] = inv_mass
    late[4, :, 0 : 2 * GT * TILE] = ghost_ref[...].astype(jnp.float32)
    late[4, :, 2 * GT * TILE :] = jnp.zeros((1, ATOMS - 2 * GT * TILE), jnp.float32)
    loads[5].wait()
    loads[6].wait()
    aux[...] = jnp.zeros((8, TILE), jnp.int32)
    aux[0:NEI, 0:TILES] = adj_ref[0]
    aux[NEI : NEI + 1, 0:TILES] = live_ref[...]

    pl.semaphore_wait(barrier, 2 + 3 * (has[0].astype(jnp.int32) + has[1].astype(jnp.int32)))
    copies = []
    for n, (step, there, comes) in enumerate(ladder):
        for side in range(2):
            to = {"rep": rep + step, "dom": dom_to[side]}
            copies.append((copy(2 * n + side, to, psend.at[side], pos_in.at[n, side]), there, comes))
    for n, (step, there, comes) in enumerate(ladder[1:]):
        to = {"rep": rep + step}
        copies.append((copy(6 + n, to, state, state_in.at[n]), there, comes))
        copies.append((copy(8 + n, to, aux, aux_in.at[n]), there, comes))
    late_copies = [
        (copy(14 + n, {"rep": rep + step}, late, late_in.at[n]), there, comes)
        for n, (step, there, comes) in enumerate(ladder[1:])
    ]
    for c, there, _ in copies + late_copies:
        when(there, c.start)
    for n in (1, 2):

        @pl.when(jnp.logical_not(ladder[n][2]))
        def _():
            pos_in[n] = jnp.zeros((2, GT, 8, TILE), jnp.float32)
            state_in[n - 1] = jnp.zeros((4, 1, ATOMS), jnp.float32)
            late_in[n - 1] = jnp.zeros((5, 1, ATOMS), jnp.float32)
            aux_in[n - 1] = jnp.zeros((8, TILE), jnp.int32)

    for i in (7, 9, 10, 11, 12, 13, 14, 15, 16):
        loads[i].wait()
    lanef = lax.broadcasted_iota(jnp.int32, (TILE, TILE), 1).astype(jnp.float32)
    row = lax.broadcasted_iota(jnp.int32, (NB, CH), 0)
    scales = jnp.zeros((NB, CH), jnp.float32)
    for b in range(NB):
        scales = jnp.where(row == b, UNFOLD[b], scales)
    vectors = jnp.concatenate([vec_ref[...], jnp.zeros((TILE - SPECIES, CH), jnp.bfloat16)], axis=0)
    partner = swap_ref[rep]
    quotient = jnp.sqrt(
        jnp.full((1, ATOMS), heat_ref[rep], jnp.float32)
        / jnp.full((1, ATOMS), heat_ref[partner], jnp.float32)
    )
    for c, there, comes in copies:
        when(there, c.wait_send)
        when(comes, c.wait_recv)

    offset = jnp.full((8, TILE), partner - rep, jnp.int32)
    aux[...] = pick(offset, aux[...], aux_in[0], aux_in[1])
    to_smem = pltpu.make_async_copy(aux, aux_smem, aux_sem)
    to_smem.start()
    for side in range(2):
        for g in range(GT):
            posext[TILES + GT * side + g] = pick(
                offset, pos_in[0, side, g], pos_in[1, side, g], pos_in[2, side, g]
            )
    offset = jnp.full((1, ATOMS), partner - rep, jnp.int32)
    for row in range(4):
        chosen[row] = pick(offset, state[row], state_in[0, row], state_in[1, row])
    for t in range(TILES):
        lanes = slice(t * TILE, (t + 1) * TILE)
        for axis in range(3):
            posext[t, axis : axis + 1, :] = chosen[axis, :, lanes]
        posext[t, 3:4, :] = chosen[3, :, lanes]
    for s in range(EXT):
        posext[s, 4:7, :] = posext[s, 0:3, :] * SCALE
    for layer in range(2):
        radial[layer] = radial_ref[layer] * scales
    for axis in range(3):
        result[axis] = chosen[axis]

    def take_late():
        for c, there, comes in late_copies:
            when(there, c.wait_send)
            when(comes, c.wait_recv)
        for row in range(5):
            chosen[4 + row] = pick(offset, late[row], late_in[0, row], late_in[1, row])

    def embed(s):
        hot = jnp.where(columns(posext[s, 3:4, :]) == lanef, 1.0, 0.0).astype(jnp.bfloat16)
        hext[s] = jnp.dot(hot, vectors, preferred_element_type=jnp.float32).astype(jnp.bfloat16)

    def fill_onehot():
        for g in range(2 * GT):
            labels = columns(chosen[8, :, g * TILE : (g + 1) * TILE])
            for t in range(TILES):
                hot = jnp.where(labels == lanef + float(t * TILE), 1.0, 0.0).astype(jnp.bfloat16)
                onehot[t, g * TILE : (g + 1) * TILE, :] = hot

    to_smem.wait()

    def fill_basis(t, buffer, slot, slots):
        if 0 in slots:
            for axis in range(3):
                xcol[t, axis] = columns(posext[t, 4 + axis : 5 + axis, :])
        for k in slots:
            far = posext[aux_smem[k, t]]
            dead = jnp.clip(k + 1 - aux_smem[NEI, t], 0, 1).astype(jnp.float32) * FAR
            xj, yj, zj = far[4:5, :] + dead, far[5:6, :], far[6:7, :]
            for c in range(TILE // CHUNK):
                rows = slice(c * CHUNK, (c + 1) * CHUNK)
                dx = xj - xcol[t, 0, rows, :]
                dy = yj - xcol[t, 1, rows, :]
                dz = zj - xcol[t, 2, rows, :]
                square = dx * dx + dy * dy + dz * dz
                a = square * lax.rsqrt(jnp.maximum(square, 1e-30))
                top = a - TOP
                g = jnp.exp2(top * (TOP - a))
                q = jnp.exp2(a * (-2.0 * ROOT))
                for b in range(NB - 1, -1, -1):
                    buffer[slot, k, b, rows, :] = g.astype(jnp.bfloat16)
                    if b:
                        g = g * q

    def sum_messages(layer, t, buffer, slot, source, parity, bs):
        if 0 in bs:
            for k in range(NEI):
                hcat[parity, k * TILE : (k + 1) * TILE, :] = source[aux_smem[k, t]]
        low, high = bs[0], bs[-1] + 1
        parts = []
        for k in range(0, NEI, 2):
            flat = jnp.concatenate(
                [
                    buffer[slot, k + i, low:high].reshape((high - low) * TILE, TILE)
                    for i in range(2)
                ],
                axis=1,
            )
            parts.append(
                jnp.dot(
                    flat,
                    hcat[parity, k * TILE : (k + 2) * TILE, :],
                    preferred_element_type=jnp.float32,
                )
            )
        summed = parts[0] + parts[1]
        weights = radial[layer]
        total = None if low == 0 else msgs[parity]
        for b in bs:
            row = b - low
            term = weights[b : b + 1, :] * summed[row * TILE : (row + 1) * TILE, :]
            total = term if total is None else total + term
        msgs[parity] = total

    def refresh(layer, t, source, parity):
        messages = msgs[parity]
        inverse = lax.rsqrt(jnp.mean(messages * messages, axis=-1, keepdims=True) + norm_eps)
        scaled = messages * inverse * gain_ref[layer : layer + 1, :]
        activation = (scaled / (1.0 + jnp.exp(-scaled))).astype(jnp.bfloat16)
        return (
            source[t].astype(jnp.float32)
            + jnp.dot(activation, mix_ref[layer], preferred_element_type=jnp.float32)
        ).astype(jnp.bfloat16)

    halves = (even, odd)

    def fill(t, u, parity, slots=range(NEI)):
        fill_basis(t, halves[parity], u, slots)

    def run_layer(layer, source, finish, prepare):
        def gather(t, u, parity, bs=range(NB)):
            sum_messages(layer, t, halves[parity], u, source, parity, bs)

        def end(t, parity):
            finish(t, refresh(layer, t, source, parity))

        if prepare:
            fill(1, 0, 1, range(0, 2))
            gather(0, 0, 0, range(0, 4))
            fill(1, 0, 1, range(2, 4))
            gather(0, 0, 0, range(4, 8))
        else:
            gather(0, 0, 0)

        def pair(u, _):
            if prepare:
                fill(2 * u + 2, u + 1, 0, range(0, 2))
                gather(2 * u + 1, u, 1, range(0, 4))
                fill(2 * u + 2, u + 1, 0, range(2, 4))
                gather(2 * u + 1, u, 1, range(4, 8))
                end(2 * u, 0)
            else:
                gather(2 * u + 1, u, 1, range(0, 4))
                end(2 * u, 0)
                gather(2 * u + 1, u, 1, range(4, 8))
            if prepare:
                fill(2 * u + 3, u + 1, 1, range(0, 2))
                gather(2 * u + 2, u + 1, 0, range(0, 4))
                fill(2 * u + 3, u + 1, 1, range(2, 4))
                gather(2 * u + 2, u + 1, 0, range(4, 8))
                end(2 * u + 1, 1)
            else:
                gather(2 * u + 2, u + 1, 0, range(0, 4))
                end(2 * u + 1, 1)
                gather(2 * u + 2, u + 1, 0, range(4, 8))
            return 0

        lax.fori_loop(0, TILES // 2 - 1, pair, 0)
        if prepare:
            take_late()
            fill_onehot()
        gather(TILES - 1, TILES // 2 - 1, 1)
        end(TILES - 2, 0)
        end(TILES - 1, 1)

    fill(0, 0, 0)
    for s in range(EXT):
        embed(s)

    def keep_mid(t, hidden):
        mid[t] = hidden

    run_layer(0, hext, keep_mid, True)

    first = 1 - jnp.minimum(lax.rem(dom, doms // 2), 1)

    def export(stage, rows, buffer, slot):
        copies = []
        for turn in range(2):
            side = lax.rem(first + turn, 2)
            to = {"dom": lax.rem(dom + 1 - 2 * side + doms, doms)}
            for g in range(GT):
                start = pl.multiple_of(((1 - side) * GT + g) * TILE, TILE)
                hot = jnp.concatenate(
                    [onehot[t, pl.ds(start, TILE), :] for t in range(TILES)], axis=1
                )
                packed = jnp.dot(hot, rows, preferred_element_type=jnp.float32)
                hsend[slot, turn, g] = packed.astype(jnp.bfloat16)
                c = copy(
                    2 * GT * stage + GT * side + g,
                    to,
                    hsend.at[slot, turn, g],
                    buffer.at[TILES + GT * side + g],
                )
                c.start()
                copies.append(c)
        return copies

    mid_copies = export(3, mid[0:TILES].reshape(ATOMS, CH), mid, 0)

    taper = [taper_ref[b] * (UNFOLD[b] * factor / SCALE) for b in range(NB)]

    def fill_lever(u, _):
        for parity in range(2):
            t = 2 * u + parity
            for k in range(NEI):
                far = posext[aux_smem[k, t]]
                for c in range(TILE // CHUNK):
                    rows = slice(c * CHUNK, (c + 1) * CHUNK)
                    total = taper[0] * halves[parity][u, k, 0, rows, :].astype(jnp.float32)
                    for b in range(1, NB):
                        total = total + taper[b] * halves[parity][u, k, b, rows, :].astype(
                            jnp.float32
                        )
                    for axis in range(3):
                        lever[t, k, axis, rows, :] = total * (
                            far[4 + axis : 5 + axis, :] - xcol[t, axis, rows, :]
                        )
        return 0

    lax.fori_loop(0, TILES // 2, fill_lever, 0)

    for c in mid_copies:
        c.wait()

    def keep_last(t, hidden):
        last[t] = hidden

    run_layer(1, mid, keep_last, False)
    key_copies = export(4, last[0:TILES].reshape(ATOMS, CH), last, 1)

    rows = last[0:TILES].reshape(ATOMS, CH)
    asked = jnp.dot(rows, target_ref[...], preferred_element_type=jnp.float32).astype(jnp.bfloat16)
    asked = lax.dot_general(
        asked, source_ref[...], (((1,), (1,)), ((), ())), preferred_element_type=jnp.float32
    )
    query[...] = asked.astype(jnp.bfloat16).reshape(TILES, TILE, CH)

    for c in key_copies:
        c.wait()

    def force_pair(u, _):
        for parity in range(2):
            t = 2 * u + parity
            for k in range(NEI):
                hcat[parity, k * TILE : (k + 1) * TILE, :] = last[aux_smem[k, t]]
            scores = lax.dot_general(
                query[t],
                hcat[parity],
                (((1,), (1,)), ((), ())),
                preferred_element_type=jnp.float32,
            )
            for axis in range(3):
                total = scores[:, 0:TILE] * lever[t, 0, axis]
                for k in range(1, NEI):
                    total = total + scores[:, k * TILE : (k + 1) * TILE] * lever[t, k, axis]
                facc[parity, axis] = total
            lanes = pl.ds(pl.multiple_of(t * TILE, TILE), TILE)
            for axis in range(3):
                result[6 + axis, :, lanes] = jnp.sum(facc[parity, axis].T, axis=0, keepdims=True)
        return 0

    lax.fori_loop(0, TILES // 2, force_pair, 0)

    for axis in range(3):
        force = result[6 + axis]
        result[3 + axis] = (chosen[4 + axis] + 0.5 * time_step * force * chosen[7]) * quotient


def hand_out(packed, pos_out, vel_out, frc_out, sem):
    copies = [
        pltpu.make_async_copy(packed.at[pl.ds(3 * i, 3)], ref, sem.at[i])
        for i, ref in enumerate((pos_out, vel_out, frc_out))
    ]
    for c in copies:
        c.start()
    for c in copies:
        c.wait()


def solution(mesh):
    reps, doms = mesh.shape["rep"], mesh.shape["dom"]

    def kernel(*refs):
        step_kernel(reps, doms, *refs)

    def local(*args):
        args = list(args)
        for i in range(3):
            args[i] = jnp.transpose(args[i], (1, 0, 2))
        args[5] = jnp.transpose(args[5], (0, 2, 1))
        vmem = pl.BlockSpec(memory_space=pltpu.VMEM)
        hbm = pl.BlockSpec(memory_space=pltpu.HBM)
        out = jax.ShapeDtypeStruct((3, 1, ATOMS), jnp.float32)
        f32, bf16 = jnp.float32, jnp.bfloat16
        scalar = (8, 14, 15, 16)
        held = [
            (pltpu.SMEM if i in scalar else pltpu.VMEM)(x.shape, x.dtype)
            for i, x in enumerate(args)
        ]
        packed = pl.pallas_call(
            kernel,
            out_shape=jax.ShapeDtypeStruct((9, 1, ATOMS), jnp.float32),
            in_specs=[hbm] * 17,
            out_specs=vmem,
            scratch_shapes=held
            + [
                pltpu.VMEM((EXT, 8, TILE), f32),
                pltpu.VMEM((2, GT, 8, TILE), f32),
                pltpu.VMEM((TILES, 3, TILE, TILE), f32),
                pltpu.VMEM((EXT, TILE, CH), bf16),
                pltpu.VMEM((EXT, TILE, CH), bf16),
                pltpu.VMEM((2, 2, GT, TILE, CH), bf16),
                pltpu.VMEM((TILES, 2 * GT * TILE, TILE), bf16),
                pltpu.VMEM((TILES // 2, NEI, NB, TILE, TILE), bf16),
                pltpu.VMEM((TILES // 2, NEI, NB, TILE, TILE), bf16),
                pltpu.VMEM((TILES, NEI, 3, TILE, TILE), f32),
                pltpu.VMEM((2, NEI * TILE, CH), bf16),
                pltpu.VMEM((2, TILE, CH), f32),
                pltpu.VMEM((2, 3, TILE, TILE), f32),
                pltpu.VMEM((EXT, TILE, CH), bf16),
                pltpu.VMEM((TILES, TILE, CH), bf16),
                pltpu.VMEM((4, 1, ATOMS), f32),
                pltpu.VMEM((5, 1, ATOMS), f32),
                pltpu.VMEM((2, 4, 1, ATOMS), f32),
                pltpu.VMEM((2, 5, 1, ATOMS), f32),
                pltpu.VMEM((3, 2, GT, 8, TILE), f32),
                pltpu.VMEM((8, TILE), jnp.int32),
                pltpu.VMEM((2, 8, TILE), jnp.int32),
                pltpu.VMEM((9, 1, ATOMS), f32),
                pltpu.SMEM((8, TILE), jnp.int32),
                pltpu.VMEM((2, NB, CH), f32),
                pltpu.SemaphoreType.DMA((17,)),
                pltpu.SemaphoreType.DMA,
                pltpu.SemaphoreType.DMA((30,)),
                pltpu.SemaphoreType.DMA((30,)),
            ],
            compiler_params=pltpu.CompilerParams(
                collective_id=0, has_side_effects=True, vmem_limit_bytes=66850000
            ),
            name="md_step",
        )(*args)
        outs = pl.pallas_call(
            hand_out,
            out_shape=(out, out, out),
            in_specs=[vmem],
            out_specs=(hbm, hbm, hbm),
            scratch_shapes=[pltpu.SemaphoreType.DMA((3,))],
            compiler_params=pltpu.CompilerParams(vmem_limit_bytes=1048576),
            name="hand_out",
        )(packed)
        return tuple(jnp.transpose(x, (1, 0, 2)) for x in outs)

    in_specs = (
        P("rep", None, "dom"),
        P("rep", None, "dom"),
        P("rep", None, "dom"),
        P("rep", "dom"),
        P("rep", "dom"),
        P("rep", "dom", None),
        P("rep", "dom"),
        P(), P(), P(), P(), P(), P(), P(), P(), P(), P(),
    )
    out_specs = (P("rep", None, "dom"), P("rep", None, "dom"), P("rep", None, "dom"))
    return jax.shard_map(local, mesh=mesh, in_specs=in_specs, out_specs=out_specs, check_vma=False)
```
